512 devices in a mesh: frow: 16 (over z_lo, y), fcol: 32 (over z_hi, x, core).
Axes of the slice: x: 4, y: 4, z: 16 (z_hi: 4, z_lo: 4; z = z_hi * 4 + z_lo), core: 2. Of those that a mesh axis runs over, the one named last changes fastest.
Arguments:
- vis: float32 [2, 131072], P(None, ('frow', 'fcol')), may hold values from -6 to 6
- station_pairs: int32 [2, 131072], P(None, ('frow', 'fcol')), may hold values from 0 to 511
- visibility_time_slot: int32 [131072], P(('frow', 'fcol')), may hold values from 0 to 15
- station_u_cells: int32 [512], replicated, may hold values from -4096 to 4095
- station_v_cells: int32 [512], replicated, may hold values from -4096 to 4095
- facet_station_gains: float32 [16, 32, 2, 8192], P('frow', 'fcol'), may hold values from -6 to 6
- holder_device_order: int32 [512], replicated, may hold values from 0 to 511, each once
Outputs:
- image: float32 [16384, 16384], P('frow', 'fcol')
The draws below stay inside these ranges and needn't reach their ends.
Inputs may be any that keep to these rules, and one draw needn't show every extreme that they name: `holder_device_order`: a permutation; its first 4 entries name distinct devices.
All inputs are finite; a program needn't handle non-finite values.
Results may differ from the reference program's by a relative error of at most 0.0037.
Values sent between devices are 32-bit elements; how exact they have to be, the bound alone decides.
A program may use at most 64 MiB of HBM per device.

```python
import math
import jax
import jax.numpy as jnp
from jax import lax

R = 1024
C = 512
M = 64
STATION_COUNT = 512
NT = 16
NBLK = 4
BLOCK_VISIBILITY = 256
IMAGE_ROW_COUNT = 16384
IMAGE_COLUMNS = 16384
N_FROW = 16
N_FCOL = 32
DEVICES = 512


def place_ends(values, rng, low, top_value):
    longest = values.shape.index(max(values.shape))
    spots = []
    for shift in (0, 1):
        where = [jax.random.randint(jax.random.fold_in(rng, axis), (), 0, length) for axis, length in enumerate(values.shape)]
        where[longest] = (where[longest] + shift) % values.shape[longest]
        spots.append(tuple(where))
    return values.at[spots[0]].set(low).at[spots[1]].set(top_value)


def level_of(own_key, dims, cuts, smallest, top_value):
    def one(dim, parts):
        draws = jax.random.uniform(jax.random.fold_in(jax.random.fold_in(own_key, 6), dim), (parts,), jnp.float32, smallest / len(cuts), top_value / len(cuts))
        return jnp.repeat(jnp.exp(draws), dims[dim] // parts).reshape((-1,) + (1,) * (len(dims) - dim - 1))

    loudness = one(*cuts[0])
    for cut in cuts[1:]:
        loudness = loudness * one(*cut)
    return loudness


def noise(own_key, dims, spread, reach, split=(), held_as=jnp.bfloat16):
    drawn = spread * jax.random.normal(own_key, dims, jnp.float32)
    if split:
        drawn = drawn * level_of(own_key, dims, split, -0.22, 0.18)
    return jnp.clip(drawn, -reach, reach).astype(held_as)


def setup_inputs(seed: int = 0) -> dict:
    seeds = jax.random.split(jax.random.key(seed), 8)
    return {
        "vis": noise(seeds[0], (2, DEVICES * BLOCK_VISIBILITY), 1.0, 6.0, ((1, 512),), jnp.float32),
        "station_pairs": place_ends(jax.random.randint(seeds[1], (2, DEVICES * BLOCK_VISIBILITY), 0, STATION_COUNT), jax.random.fold_in(seeds[1], 1), 0, STATION_COUNT - 1).astype(jnp.int32),
        "visibility_time_slot": place_ends(jax.random.randint(seeds[2], (DEVICES * BLOCK_VISIBILITY,), 0, NT), jax.random.fold_in(seeds[2], 1), 0, NT - 1).astype(jnp.int32),
        "station_u_cells": place_ends(jax.random.randint(seeds[3], (STATION_COUNT,), 0 - IMAGE_ROW_COUNT // 4, IMAGE_ROW_COUNT // 4), jax.random.fold_in(seeds[3], 1), 0 - IMAGE_ROW_COUNT // 4, (IMAGE_ROW_COUNT // 4) - 1).astype(jnp.int32),
        "station_v_cells": place_ends(jax.random.randint(seeds[4], (STATION_COUNT,), 0 - IMAGE_COLUMNS // 4, IMAGE_COLUMNS // 4), jax.random.fold_in(seeds[4], 1), 0 - IMAGE_COLUMNS // 4, (IMAGE_COLUMNS // 4) - 1).astype(jnp.int32),
        "facet_station_gains": noise(seeds[5], (N_FROW, N_FCOL, 2, STATION_COUNT * NT), 1.0, 6.0, ((0, 16), (1, 32)), jnp.float32),
        "holder_device_order": jax.random.permutation(seeds[6], DEVICES).astype(jnp.int32),
    }


def taper_line(length):
    index = jnp.arange(length + 2 * M, dtype=jnp.int32).astype(jnp.float32)
    rising = (index + 0.5) / (2.0 * M)
    falling = (length + 2 * M - index - 0.5) / (2.0 * M)
    return jnp.minimum(jnp.minimum(rising, falling), 1.0)

def phase_angles(freq, pixels, modulus):
    cells = jnp.mod(freq, modulus)[None, :] * jnp.mod(pixels, modulus)[:, None] % modulus
    return cells.astype(jnp.float32) * (2.0 * math.pi / modulus)

def block_weights(values, baseline_pairs, slots, g_tab, scale):
    first = baseline_pairs[0] * NT + slots
    second = baseline_pairs[1] * NT + slots
    g1r = g_tab[0][first]
    g1i = g_tab[1][first]
    g2r = g_tab[0][second]
    g2i = g_tab[1][second]
    real_gain = g1r * g2r + g1i * g2i
    imag_gain = g1i * g2r - g1r * g2i
    wreal = scale * (values[0] * real_gain - values[1] * imag_gain)
    wimag = scale * (values[0] * imag_gain + values[1] * real_gain)
    return (wreal, wimag)

def reference(vis, station_pairs, visibility_time_slot, station_u_cells, station_v_cells, facet_station_gains, holder_device_order):
    n_rows = R * N_FROW
    n_cols = C * N_FCOL
    values, baseline_pairs, slots = ([], [], [])
    for step in range(NBLK):
        start_offset = (holder_device_order[step] * BLOCK_VISIBILITY).astype(jnp.int32)
        zero_value = jnp.zeros((), jnp.int32)
        values.append(lax.dynamic_slice(vis, (zero_value, start_offset), (2, BLOCK_VISIBILITY)))
        baseline_pairs.append(lax.dynamic_slice(station_pairs, (zero_value, start_offset), (2, BLOCK_VISIBILITY)))
        slots.append(lax.dynamic_slice(visibility_time_slot, (start_offset,), (BLOCK_VISIBILITY,)))
    values = jnp.concatenate(values, 1)
    baseline_pairs = jnp.concatenate(baseline_pairs, 1)
    slots = jnp.concatenate(slots, 0)
    frequency_u = station_u_cells[baseline_pairs[0]] - station_u_cells[baseline_pairs[1]]
    frequency_v = station_v_cells[baseline_pairs[0]] - station_v_cells[baseline_pairs[1]]
    scale = 0.5 / math.sqrt(NBLK * BLOCK_VISIBILITY)
    row_taper = taper_line(R)
    col_taper = taper_line(C)
    canvas = jnp.zeros((n_rows + 2 * M, n_cols + 2 * M), jnp.float32)

    def one_facet(flat, canvas):
        frow_at = (flat // N_FCOL).astype(jnp.int32)
        fcol_at = (flat % N_FCOL).astype(jnp.int32)
        g_tab = facet_station_gains[frow_at, fcol_at]
        wreal, wimag = block_weights(values, baseline_pairs, slots, g_tab, scale)
        rows = frow_at * R - M + jnp.arange(R + 2 * M, dtype=jnp.int32)
        cols = fcol_at * C - M + jnp.arange(C + 2 * M, dtype=jnp.int32)
        theta = phase_angles(frequency_u, rows, n_rows)
        phi = phase_angles(frequency_v, cols, n_cols).T
        row_table = jnp.concatenate([jnp.cos(theta), jnp.sin(theta)], 1).astype(jnp.bfloat16)
        top = wreal[:, None] * jnp.cos(phi) - wimag[:, None] * jnp.sin(phi)
        bottom = -(wimag[:, None] * jnp.cos(phi) + wreal[:, None] * jnp.sin(phi))
        col_table = jnp.concatenate([top, bottom], 0).astype(jnp.bfloat16)
        facet = jnp.dot(row_table.astype(jnp.float32), col_table.astype(jnp.float32), precision=lax.Precision.HIGHEST)
        tapered = facet * row_taper[:, None] * col_taper[None, :]
        corner = (frow_at * R, fcol_at * C)
        current = lax.dynamic_slice(canvas, corner, (R + 2 * M, C + 2 * M))
        return lax.dynamic_update_slice(canvas, current + tapered, corner)
    canvas = lax.fori_loop(0, N_FROW * N_FCOL, one_facet, canvas)
    return canvas[M:M + n_rows, M:M + n_cols]
```

```python
import math

import jax
import jax.numpy as jnp
from jax import lax
from jax.experimental import pallas as pl
from jax.experimental.pallas import tpu as pltpu
from jax.sharding import PartitionSpec as P

R = 1024
C = 512
M = 64
NT = 16
NBLK = 4
BLOCK = 256
K = NBLK * BLOCK
N_FROW = 16
N_FCOL = 32
LANES = 128
SUB = 8
GROUPS = K // LANES
SIZE = R * N_FROW
PLANE = 32
DEPTH = 16
PIECES = 10
GAIN_ROWS = 64
MESH = pl.DeviceIdType.MESH
AROUND = [(dr, dc) for dr in (-1, 0, 1) for dc in (-1, 0, 1) if (dr, dc) != (0, 0)]


def place(dr, dc):
    return (1 + dr) * 3 + 1 + dc


def exchange_kernel(
    order_ref, vis_ref, pairs_ref, slot_ref, gains_ref, out_ref, around_ref,
    pay, raw, part, line, done, send1, recv1, send2, recv2, send3, recv3, send_g, recv_g,
):
    fr, fc = lax.axis_index("frow"), lax.axis_index("fcol")
    z_lo, y = fr // 4, fr % 4
    z_hi, xc = fc // 8, fc % 8
    me = y * 8 + xc
    my_z = z_hi * 4 + z_lo
    mine = me // 3
    reduces = jnp.logical_and(me % 3 == 0, mine < PIECES)

    def in_plane(s):
        return (z_lo * 4 + s // 8, z_hi * 8 + s % 8)

    def in_line(z):
        return ((z % 4) * 4 + y, (z // 4) * 8 + xc)

    def inside(dr, dc):
        row, col = fr + dr, fc + dc
        return (row >= 0) & (row < N_FROW) & (col >= 0) & (col < N_FCOL)

    barrier = pltpu.get_barrier_semaphore()

    def greet_plane(t, carry):
        pl.semaphore_signal(barrier, inc=1, device_id=in_plane((me + t) % PLANE), device_id_type=MESH)
        return carry

    lax.fori_loop(1, PLANE, greet_plane, 0)

    @pl.when(reduces)
    def _():
        def greet_line(t, carry):
            pl.semaphore_signal(barrier, inc=1, device_id=in_line((my_z + t) % DEPTH), device_id_type=MESH)
            return carry

        lax.fori_loop(1, DEPTH, greet_line, 0)

    count = PLANE - 1 + jnp.where(reduces, DEPTH - 1, 0)
    for dr, dc in AROUND:
        count = count + inside(dr, dc).astype(jnp.int32)

        @pl.when(inside(dr, dc))
        def _():
            pl.semaphore_signal(barrier, inc=1, device_id=(fr + dr, fc + dc), device_id_type=MESH)

    for half in range(2):
        cols = slice(half * LANES, (half + 1) * LANES)
        pay[half] = vis_ref[0:1, cols]
        pay[2 + half] = vis_ref[1:2, cols]
        pay[4 + half] = pairs_ref[0:1, cols].astype(jnp.float32)
        pay[6 + half] = pairs_ref[1:2, cols].astype(jnp.float32)
        pay[8 + half] = slot_ref[0:1, cols].astype(jnp.float32)

    pl.semaphore_wait(barrier, count)

    def piece_copy(j):
        return pltpu.make_async_remote_copy(
            src_ref=pay.at[j], dst_ref=raw.at[me], send_sem=send1.at[j], recv_sem=recv1.at[me],
            device_id=in_plane(3 * j), device_id_type=MESH,
        )

    def gain_copy(dr, dc):
        return pltpu.make_async_remote_copy(
            src_ref=gains_ref, dst_ref=around_ref.at[place(-dr, -dc)],
            send_sem=send_g.at[place(dr, dc)], recv_sem=recv_g.at[place(-dr, -dc)],
            device_id=(fr + dr, fc + dc), device_id_type=MESH,
        )

    for j in range(PIECES):
        @pl.when(me != 3 * j)
        def _():
            piece_copy(j).start()

    for dr, dc in AROUND:
        @pl.when(inside(dr, dc))
        def _():
            gain_copy(dr, dc).start()

    def line_copy(t):
        return pltpu.make_async_remote_copy(
            src_ref=part, dst_ref=line.at[my_z], send_sem=send2.at[t], recv_sem=recv2.at[my_z],
            device_id=in_line((my_z + t) % DEPTH), device_id_type=MESH,
        )

    def done_copy(t):
        return pltpu.make_async_remote_copy(
            src_ref=done.at[mine], dst_ref=done.at[mine], send_sem=send3.at[t], recv_sem=recv3.at[mine],
            device_id=in_plane((me + t) % PLANE), device_id_type=MESH,
        )

    @pl.when(reduces)
    def _():
        raw[me] = pay[mine]

        def arrived(t, carry):
            s = (me + t) % PLANE
            pltpu.make_async_copy(raw.at[s], raw.at[s], recv1.at[s]).wait()
            return carry

        lax.fori_loop(1, PLANE, arrived, 0)
        s = lax.broadcasted_iota(jnp.int32, (PLANE, 1, LANES), 0)
        holder = (z_lo * 4 + s // 8) * N_FCOL + z_hi * 8 + s % 8
        values = raw[...]
        for b in range(NBLK):
            part[b : b + 1, :] = jnp.sum(jnp.where(holder == order_ref[b], values, 0.0), axis=0)

        def start_line(t, carry):
            line_copy(t).start()
            return carry

        lax.fori_loop(1, DEPTH, start_line, 0)
        line[my_z] = part[...]

        def line_arrived(t, carry):
            z = (my_z + t) % DEPTH
            pltpu.make_async_copy(line.at[z], line.at[z], recv2.at[z]).wait()
            return carry

        lax.fori_loop(1, DEPTH, line_arrived, 0)
        done[mine] = jnp.sum(line[...], axis=0)

        def start_done(t, carry):
            done_copy(t).start()
            return carry

        lax.fori_loop(1, PLANE, start_done, 0)

    for j in range(PIECES):
        @pl.when(me != 3 * j)
        def _():
            pltpu.make_async_copy(done.at[j], done.at[j], recv3.at[j]).wait()

    out_ref[...] = done[...]

    for j in range(PIECES):
        @pl.when(me != 3 * j)
        def _():
            piece_copy(j).wait_send()

    @pl.when(reduces)
    def _():
        def sent_line(t, carry):
            line_copy(t).wait_send()
            return carry

        def sent_done(t, carry):
            done_copy(t).wait_send()
            return carry

        lax.fori_loop(1, DEPTH, sent_line, 0)
        lax.fori_loop(1, PLANE, sent_done, 0)

    for dr, dc in AROUND:
        @pl.when(inside(dr, dc))
        def _():
            gain_copy(dr, dc).wait_send()
            slot = around_ref.at[place(dr, dc)]
            pltpu.make_async_copy(slot, slot, recv_g.at[place(dr, dc)]).wait()


def exchange(order, vis, pairs, slot, gains):
    vmem = pl.BlockSpec(memory_space=pltpu.VMEM)
    anywhere = pl.BlockSpec(memory_space=pl.ANY)
    dma = pltpu.SemaphoreType.DMA
    return pl.pallas_call(
        exchange_kernel,
        out_shape=(
            jax.ShapeDtypeStruct((PIECES, NBLK, LANES), jnp.float32),
            jax.ShapeDtypeStruct((9, GAIN_ROWS, 2, LANES), jnp.float32),
        ),
        in_specs=[pl.BlockSpec(memory_space=pltpu.SMEM), vmem, vmem, vmem, anywhere],
        out_specs=(vmem, anywhere),
        scratch_shapes=[
            pltpu.VMEM((PIECES, 1, LANES), jnp.float32),
            pltpu.VMEM((PLANE, 1, LANES), jnp.float32),
            pltpu.VMEM((NBLK, LANES), jnp.float32),
            pltpu.VMEM((DEPTH, NBLK, LANES), jnp.float32),
            pltpu.VMEM((PIECES, NBLK, LANES), jnp.float32),
            dma((PIECES,)), dma((PLANE,)), dma((DEPTH,)), dma((DEPTH,)),
            dma((PLANE,)), dma((PIECES,)), dma((9,)), dma((9,)),
        ],
        compiler_params=pltpu.CompilerParams(collective_id=0, has_side_effects=True),
        name="exchange",
    )(order, vis, pairs, slot, gains)


def circle(m):
    m = m & (2 * SIZE - 1)
    quarter = (m + SIZE // 4) >> 13
    x = (m - (quarter << 13)).astype(jnp.float32) * (math.pi / SIZE)
    x2 = x * x
    s = x * (1.0 + x2 * (-1 / 6 + x2 * (1 / 120 + x2 * (-1 / 5040 + x2 * (1 / 362880)))))
    c = 1.0 + x2 * (-1 / 2 + x2 * (1 / 24 + x2 * (-1 / 720 + x2 * (1 / 40320))))
    odd = (quarter & 1) == 1
    cos = jnp.where(odd, s, c)
    sin = jnp.where(odd, c, s)
    cos = jnp.where(((quarter + 1) & 2) == 2, -cos, cos)
    sin = jnp.where((quarter & 2) == 2, -sin, sin)
    return cos, sin


def take_lanes(row, index):
    return jnp.take_along_axis(row, index, axis=1, mode="promise_in_bounds")


HALF = R // 2
LOW = 32
HIGH = C // LOW
WIDE = 256
SETS = ((3, 4, 5), (0, 1, 2), (6, 7, 8))


def image_kernel(
    fin_ref, ucell_ref, vcell_ref, own_ref, around_ref, out_ref,
    w_scr, uv_scr, wave_u, wave_v, front, rows_c, rows_s, cols_a, cols_b,
):
    fr, fc = lax.axis_index("frow"), lax.axis_index("fcol")
    f32, i32 = jnp.float32, jnp.int32
    s1 = fin_ref[2].astype(i32)
    s2 = fin_ref[3].astype(i32)
    t = fin_ref[4].astype(i32)

    def station(ref):
        total = jnp.zeros((SUB, LANES), i32)
        for row in range(4):
            cells = jnp.broadcast_to(ref[row : row + 1, :], (SUB, LANES))
            one = take_lanes(cells, s1 & 127)
            two = take_lanes(cells, s2 & 127)
            total = total + jnp.where((s1 >> 7) == row, one, 0) - jnp.where((s2 >> 7) == row, two, 0)
        return total

    uv_scr[0] = station(ucell_ref)
    uv_scr[1] = station(vcell_ref)

    first, second = s1 * NT + t, s2 * NT + t
    lo1, hi1 = first & 127, first >> 7
    lo2, hi2 = second & 127, second >> 7

    def gather_row(row, carry):
        here1, here2 = hi1 == row, hi2 == row
        found = []
        for f in range(9):
            for part in range(2):
                where = 2 * row + part
                line = own_ref[pl.ds(where, 1), :] if f == 4 else around_ref[f, pl.ds(where, 1), :]
                line = jnp.broadcast_to(line, (SUB, LANES))
                a, b = carry[2 * len(found)], carry[2 * len(found) + 1]
                found.append((jnp.where(here1, take_lanes(line, lo1), a), jnp.where(here2, take_lanes(line, lo2), b)))
        return tuple(x for pair in found for x in pair)

    zero = jnp.zeros((SUB, LANES), f32)
    gains = lax.fori_loop(0, GAIN_ROWS, gather_row, (zero,) * 36)
    scale = 0.5 / math.sqrt(K)
    v_r, v_i = fin_ref[0], fin_ref[1]
    for f in range(9):
        g1r, g2r, g1i, g2i = gains[4 * f : 4 * f + 4]
        real_gain = g1r * g2r + g1i * g2i
        imag_gain = g1i * g2r - g1r * g2i
        w_r = scale * (v_r * real_gain - v_i * imag_gain)
        w_i = scale * (v_r * imag_gain + v_i * real_gain)
        row, col = fr + f // 3 - 1, fc + f % 3 - 1
        inside = (row >= 0) & (row < N_FROW) & (col >= 0) & (col < N_FCOL)
        w_scr[2 * f] = jnp.where(inside, w_r, 0.0)
        w_scr[2 * f + 1] = jnp.where(inside, w_i, 0.0)

    centre = fr * (2 * R) + R - 1
    low = lax.broadcasted_iota(i32, (LOW, LANES), 0)
    high = lax.broadcasted_iota(i32, (HIGH, LANES), 0)

    def tables(g, carry):
        lanes = pl.ds(pl.multiple_of(g * LANES, LANES), LANES)
        u = uv_scr[0, pl.ds(g, 1), :]
        v = uv_scr[1, pl.ds(g, 1), :]
        lc, ls = circle(u * (2 * low + 1))
        hc, hs = circle(u * (2 * LOW * high))
        wave_u[0] = hc
        wave_u[1] = hs
        for h in range(HIGH):
            bc, bs = wave_u[0, h : h + 1, :], wave_u[1, h : h + 1, :]
            rows_c[h * LOW : (h + 1) * LOW, lanes] = (bc * lc - bs * ls).astype(jnp.bfloat16)
            rows_s[h * LOW : (h + 1) * LOW, lanes] = (bc * ls + bs * lc).astype(jnp.bfloat16)
        lc, ls = circle(v * (2 * low))
        wave_v[0, g] = lc
        wave_v[1, g] = ls
        pc, ps = circle(u * centre + v * (2 * (fc * C + LOW * high)))
        for f in range(9):
            w_r, w_i = w_scr[2 * f, pl.ds(g, 1), :], w_scr[2 * f + 1, pl.ds(g, 1), :]
            front[2 * f, g] = w_r * pc - w_i * ps
            front[2 * f + 1, g] = w_r * ps + w_i * pc
        return carry

    lax.fori_loop(0, GROUPS, tables, 0)

    lowf = low.astype(f32)

    def columns(chunk):
        def group(g, carry):
            lanes = pl.ds(pl.multiple_of(g * LANES, LANES), LANES)
            lc, ls = wave_v[0, g], wave_v[1, g]
            for n, (left, mid, right) in enumerate(SETS):
                for i in range(WIDE // LOW):
                    h = chunk * (WIDE // LOW) + i
                    w_r, w_i = front[2 * mid, g, h : h + 1, :], front[2 * mid + 1, g, h : h + 1, :]
                    if h * LOW < M or h * LOW >= C - M:
                        if h * LOW < M:
                            side = left
                            t_mid = (lowf + (h * LOW + M + 0.5)) * (1 / (2 * M))
                            t_side = (M - 0.5 - h * LOW - lowf) * (1 / (2 * M))
                        else:
                            side = right
                            t_mid = (C + M - 0.5 - h * LOW - lowf) * (1 / (2 * M))
                            t_side = (lowf + (h * LOW - C + M + 0.5)) * (1 / (2 * M))
                        w_r = t_mid * w_r + t_side * front[2 * side, g, h : h + 1, :]
                        w_i = t_mid * w_i + t_side * front[2 * side + 1, g, h : h + 1, :]
                    at = slice(i * LOW, (i + 1) * LOW)
                    cols_a[n, at, lanes] = (w_r * lc - w_i * ls).astype(jnp.bfloat16)
                    cols_b[n, at, lanes] = (w_r * ls + w_i * lc).astype(jnp.bfloat16)
            return carry

        lax.fori_loop(0, GROUPS, group, 0)

    def times(rows, cols):
        return lax.dot_general(rows, cols, (((1,), (1,)), ((), ())), preferred_element_type=f32)

    edge = HALF - M
    d = lax.broadcasted_iota(i32, (M, 1), 0).astype(f32)
    t_own = (2 * M - 0.5 - M - d + M) * (1 / (2 * M))
    t_next = (d + 0.5) * (1 / (2 * M))
    turn = SUB - 1 - lax.broadcasted_iota(i32, (SUB, LANES), 0)

    for chunk in range(C // WIDE):
        columns(chunk)
        at = slice(chunk * WIDE, (chunk + 1) * WIDE)
        even = times(rows_c[...], cols_a[0])
        odd = times(rows_s[...], cols_b[0])
        edge_c, edge_s = rows_c[edge:, :], rows_s[edge:, :]
        above = times(edge_c, cols_a[1]) + times(edge_s, cols_b[1])
        below = times(edge_c, cols_a[2]) - times(edge_s, cols_b[2])
        down = even - odd
        up = even + odd
        out_ref[HALF : R - M, at] = down[:edge]
        out_ref[R - M :, at] = down[edge:] * t_own + below * t_next
        up = jnp.concatenate([up[:edge], up[edge:] * t_own + above * t_next], 0)
        for i in range(HALF // SUB):
            for k in range(WIDE // LANES):
                tile = up[i * SUB : (i + 1) * SUB, k * LANES : (k + 1) * LANES]
                tile = jnp.take_along_axis(tile, turn, axis=0, mode="promise_in_bounds")
                out_ref[HALF - (i + 1) * SUB : HALF - i * SUB, chunk * WIDE + k * LANES : chunk * WIDE + (k + 1) * LANES] = tile


def image_of(fin, ucell, vcell, own, around):
    vmem = pl.BlockSpec(memory_space=pltpu.VMEM)
    return pl.pallas_call(
        image_kernel,
        out_shape=jax.ShapeDtypeStruct((R, C), jnp.float32),
        in_specs=[vmem] * 5,
        out_specs=vmem,
        scratch_shapes=[
            pltpu.VMEM((18, SUB, LANES), jnp.float32),
            pltpu.VMEM((2, SUB, LANES), jnp.int32),
            pltpu.VMEM((2, HIGH, LANES), jnp.float32),
            pltpu.VMEM((2, GROUPS, LOW, LANES), jnp.float32),
            pltpu.VMEM((18, GROUPS, HIGH, LANES), jnp.float32),
            pltpu.VMEM((HALF, K), jnp.bfloat16),
            pltpu.VMEM((HALF, K), jnp.bfloat16),
            pltpu.VMEM((3, WIDE, K), jnp.bfloat16),
            pltpu.VMEM((3, WIDE, K), jnp.bfloat16),
        ],
        compiler_params=pltpu.CompilerParams(vmem_limit_bytes=48 * 1024 * 1024),
        name="image",
    )(fin, ucell, vcell, own, around)


def shards(vis, station_pairs, visibility_time_slot, station_u_cells, station_v_cells, facet_station_gains, holder_device_order):
    gains = facet_station_gains.reshape(2, GAIN_ROWS, LANES).transpose(1, 0, 2)
    fin, around = exchange(holder_device_order, vis, station_pairs, visibility_time_slot.reshape(1, BLOCK), gains)
    return image_of(
        fin.reshape(5, 2 * NBLK, LANES),
        station_u_cells.reshape(4, LANES),
        station_v_cells.reshape(4, LANES),
        gains.reshape(2 * GAIN_ROWS, LANES),
        around.reshape(9, 2 * GAIN_ROWS, LANES),
    )


def solution(mesh):
    return jax.shard_map(
        shards,
        mesh=mesh,
        in_specs=(
            P(None, ("frow", "fcol")),
            P(None, ("frow", "fcol")),
            P(("frow", "fcol")),
            P(),
            P(),
            P("frow", "fcol", None, None),
            P(),
        ),
        out_specs=P("frow", "fcol"),
        check_vma=False,
    )
```

```python
import math

import jax
import jax.numpy as jnp
from jax import lax
from jax.experimental import pallas as pl
from jax.experimental.pallas import tpu as pltpu
from jax.sharding import PartitionSpec as P

R = 1024
C = 512
M = 64
NT = 16
NBLK = 4
BLOCK = 256
K = NBLK * BLOCK
N_FROW = 16
N_FCOL = 32
LANES = 128
SUB = 8
GROUPS = K // LANES
SIZE = R * N_FROW
PLANE = 32
DEPTH = 16
PIECES = 10
GAIN_ROWS = 64
MESH = pl.DeviceIdType.MESH
AROUND = [(dr, dc) for dr in (-1, 0, 1) for dc in (-1, 0, 1) if (dr, dc) != (0, 0)]


def place(dr, dc):
    return (1 + dr) * 3 + 1 + dc


def circle(m):
    m = m & (2 * SIZE - 1)
    quarter = (m + SIZE // 4) >> 13
    x = (m - (quarter << 13)).astype(jnp.float32) * (math.pi / SIZE)
    x2 = x * x
    s = x * (1.0 + x2 * (-1 / 6 + x2 * (1 / 120 + x2 * (-1 / 5040 + x2 * (1 / 362880)))))
    c = 1.0 + x2 * (-1 / 2 + x2 * (1 / 24 + x2 * (-1 / 720 + x2 * (1 / 40320))))
    odd = (quarter & 1) == 1
    cos = jnp.where(odd, s, c)
    sin = jnp.where(odd, c, s)
    cos = jnp.where(((quarter + 1) & 2) == 2, -cos, cos)
    sin = jnp.where((quarter & 2) == 2, -sin, sin)
    return cos, sin


def take_lanes(row, index):
    return jnp.take_along_axis(row, index, axis=1, mode="promise_in_bounds")


def exchange_kernel(
    order_hbm, vis_hbm, pairs_hbm, slot_hbm, ucell_hbm, vcell_hbm, gain_hbm, uv_ref, w_ref,
    order, vis, pairs, slot, ucell, vcell, gain, pay, raw, part, line, done, w_own, w_all,
    in_sem, send1, recv1, send2, recv2, send3, recv3, send_w, recv_w,
):
    fr, fc = lax.axis_index("frow"), lax.axis_index("fcol")
    f32, i32 = jnp.float32, jnp.int32
    z_lo, y = lax.div(fr, 4), lax.rem(fr, 4)
    z_hi, xc = lax.div(fc, 8), lax.rem(fc, 8)
    me = y * 8 + xc
    my_z = z_hi * 4 + z_lo
    mine = lax.div(me, 3)
    reduces = jnp.logical_and(lax.rem(me, 3) == 0, mine < PIECES)
    plane_row, plane_col = z_lo * 4, z_hi * 8

    def in_plane(s):
        return (plane_row + s // 8, plane_col + s % 8)

    def in_line(z):
        return ((z % 4) * 4 + y, (z // 4) * 8 + xc)

    def inside(dr, dc):
        row, col = fr + dr, fc + dc
        return (row >= 0) & (row < N_FROW) & (col >= 0) & (col < N_FCOL)

    barrier = pltpu.get_barrier_semaphore()

    def greet(device):
        pl.semaphore_signal(barrier, inc=1, device_id=device, device_id_type=MESH)

    @pl.when(reduces)
    def _():
        for z in range(DEPTH):
            @pl.when(my_z != z)
            def _():
                greet(in_line(z))

        for s in range(PLANE):
            @pl.when(me != s)
            def _():
                greet(in_plane(s))

    @pl.when(jnp.logical_not(reduces))
    def _():
        for j in range(PIECES):
            greet(in_plane(3 * j))

    count = jnp.where(reduces, PLANE - 1 + DEPTH - 1, PIECES)
    for dr, dc in AROUND:
        count = count + inside(dr, dc).astype(i32)

        @pl.when(inside(dr, dc))
        def _():
            greet((fr + dr, fc + dc))

    loads = ((vis_hbm, vis), (pairs_hbm, pairs), (slot_hbm, slot), (order_hbm, order), (ucell_hbm, ucell), (vcell_hbm, vcell), (gain_hbm, gain))
    loads = [pltpu.make_async_copy(a, b, in_sem.at[n]) for n, (a, b) in enumerate(loads)]
    for load in loads:
        load.start()
    for dr, dc in AROUND:
        @pl.when(jnp.logical_not(inside(dr, dc)))
        def _():
            w_all[place(dr, dc)] = jnp.zeros((2, SUB, LANES), f32)

    for load in loads:
        load.wait()
    for half in range(2):
        cols = slice(half * LANES, (half + 1) * LANES)
        pay[half] = vis[0:1, cols]
        pay[2 + half] = vis[1:2, cols]
        pay[4 + half] = pairs[0:1, cols].astype(f32)
        pay[6 + half] = pairs[1:2, cols].astype(f32)
        pay[8 + half] = slot[0:1, cols].astype(f32)

    pl.semaphore_wait(barrier, count)

    def piece_copy(j):
        return pltpu.make_async_remote_copy(
            src_ref=pay.at[j], dst_ref=raw.at[me], send_sem=send1.at[j], recv_sem=recv1,
            device_id=in_plane(3 * j), device_id_type=MESH,
        )

    def line_copy(z):
        return pltpu.make_async_remote_copy(
            src_ref=part, dst_ref=line.at[my_z], send_sem=send2.at[z], recv_sem=recv2,
            device_id=in_line(z), device_id_type=MESH,
        )

    def done_copy(s):
        return pltpu.make_async_remote_copy(
            src_ref=done.at[mine], dst_ref=done.at[mine], send_sem=send3.at[s], recv_sem=recv3,
            device_id=in_plane(s), device_id_type=MESH,
        )

    def weight_copy(dr, dc):
        return pltpu.make_async_remote_copy(
            src_ref=w_own, dst_ref=w_all.at[place(-dr, -dc)],
            send_sem=send_w.at[place(dr, dc)], recv_sem=recv_w.at[place(-dr, -dc)],
            device_id=(fr + dr, fc + dc), device_id_type=MESH,
        )

    def landed(ref, slots, sem):
        view = ref.at[pl.ds(0, slots)]
        pltpu.make_async_copy(view, view, sem).wait()

    for j in range(PIECES):
        @pl.when(me != 3 * j)
        def _():
            piece_copy(j).start()

    @pl.when(reduces)
    def _():
        raw[me] = pay[mine]
        s = lax.broadcasted_iota(i32, (PLANE, 1, LANES), 0)
        holder = (plane_row + (s >> 3)) * N_FCOL + plane_col + (s & 7)
        landed(raw, PLANE - 1, recv1)
        values = raw[...]
        for b in range(NBLK):
            part[b : b + 1, :] = jnp.sum(jnp.where(holder == order[b], values, 0.0), axis=0)
        for z in range(DEPTH):
            @pl.when(my_z != z)
            def _():
                line_copy(z).start()

        line[my_z] = part[...]
        landed(line, DEPTH - 1, recv2)
        done[mine] = jnp.sum(line[...], axis=0)
        for s in range(PLANE):
            @pl.when(me != s)
            def _():
                done_copy(s).start()

        landed(done, PIECES - 1, recv3)

    @pl.when(jnp.logical_not(reduces))
    def _():
        landed(done, PIECES, recv3)

    def value(v):
        return jnp.concatenate([done[2 * v], done[2 * v + 1]], 0)

    s1, s2, t = value(2).astype(i32), value(3).astype(i32), value(4).astype(i32)
    first, second = s1 * NT + t, s2 * NT + t

    def pick(part, index):
        lane, row = index & 127, index >> 7
        bits = [(row & (1 << b)) != 0 for b in range(6)]
        stack = []
        for n in range(GAIN_ROWS):
            values = jnp.broadcast_to(gain[2 * n + part : 2 * n + part + 1, :], (SUB, LANES))
            found, level = take_lanes(values, lane), 0
            while stack and stack[-1][0] == level:
                found = jnp.where(bits[level], found, stack.pop()[1])
                level += 1
            stack.append((level, found))
        return stack[0][1]

    scale = 0.5 / math.sqrt(K)
    v_r, v_i = value(0), value(1)
    g1r, g1i = pick(0, first), pick(1, first)
    g2r, g2i = pick(0, second), pick(1, second)
    real_gain = g1r * g2r + g1i * g2i
    imag_gain = g1i * g2r - g1r * g2i
    w_own[0] = scale * (v_r * real_gain - v_i * imag_gain)
    w_own[1] = scale * (v_r * imag_gain + v_i * real_gain)
    for dr, dc in AROUND:
        @pl.when(inside(dr, dc))
        def _():
            weight_copy(dr, dc).start()

    def station(ref):
        total = jnp.zeros((SUB, LANES), i32)
        for row in range(4):
            cells = jnp.broadcast_to(ref[row : row + 1, :], (SUB, LANES))
            one = take_lanes(cells, s1 & 127)
            two = take_lanes(cells, s2 & 127)
            total = total + jnp.where((s1 >> 7) == row, one, 0) - jnp.where((s2 >> 7) == row, two, 0)
        return total

    u, v = station(ucell), station(vcell)
    uv_ref[0] = u
    uv_ref[1] = v
    mid_c, mid_s = circle(u * (fr * (2 * R) + R - 1) + v * (2 * (fc * C + C // 2)))

    def turn(place_of, w_r, w_i):
        w_ref[2 * place_of] = w_r * mid_c - w_i * mid_s
        w_ref[2 * place_of + 1] = w_r * mid_s + w_i * mid_c

    turn(4, w_own[0], w_own[1])

    for j in range(PIECES):
        @pl.when(me != 3 * j)
        def _():
            piece_copy(j).wait_send()

    @pl.when(reduces)
    def _():
        for z in range(DEPTH):
            @pl.when(my_z != z)
            def _():
                line_copy(z).wait_send()

        for s in range(PLANE):
            @pl.when(me != s)
            def _():
                done_copy(s).wait_send()

    for dr, dc in AROUND:
        @pl.when(inside(dr, dc))
        def _():
            weight_copy(dr, dc).wait_send()
            slot_of = w_all.at[place(dr, dc)]
            pltpu.make_async_copy(slot_of, slot_of, recv_w.at[place(dr, dc)]).wait()

    for dr, dc in AROUND:
        turn(place(dr, dc), w_all[place(dr, dc), 0], w_all[place(dr, dc), 1])


def exchange(order, vis, pairs, slot, ucell, vcell, gain):
    vmem = pl.BlockSpec(memory_space=pltpu.VMEM)
    dma = pltpu.SemaphoreType.DMA
    f32, i32 = jnp.float32, jnp.int32
    return pl.pallas_call(
        exchange_kernel,
        out_shape=(jax.ShapeDtypeStruct((2, SUB, LANES), i32), jax.ShapeDtypeStruct((18, SUB, LANES), f32)),
        in_specs=[pl.BlockSpec(memory_space=pl.ANY)] * 7,
        out_specs=(vmem, vmem),
        scratch_shapes=[
            pltpu.SMEM((N_FROW * N_FCOL,), i32),
            pltpu.VMEM((2, BLOCK), f32),
            pltpu.VMEM((2, BLOCK), i32),
            pltpu.VMEM((1, BLOCK), i32),
            pltpu.VMEM((4, LANES), i32),
            pltpu.VMEM((4, LANES), i32),
            pltpu.VMEM((2 * GAIN_ROWS, LANES), f32),
            pltpu.VMEM((PIECES, 1, LANES), f32),
            pltpu.VMEM((PLANE, 1, LANES), f32),
            pltpu.VMEM((NBLK, LANES), f32),
            pltpu.VMEM((DEPTH, NBLK, LANES), f32),
            pltpu.VMEM((PIECES, NBLK, LANES), f32),
            pltpu.VMEM((2, SUB, LANES), f32),
            pltpu.VMEM((9, 2, SUB, LANES), f32),
            dma((7,)), dma((PIECES,)), dma, dma((DEPTH,)), dma, dma((PLANE,)), dma, dma((9,)), dma((9,)),
        ],
        compiler_params=pltpu.CompilerParams(collective_id=0, has_side_effects=True),
        name="exchange",
    )(order, vis, pairs, slot, ucell, vcell, gain)


HALF = R // 2
LOW = 32
WIDE = 256
EDGE = HALF - M
INNER = tuple(range(-4, 4))
OUTER = tuple(range(-8, -4)) + tuple(range(4, 8))


def image_kernel(
    uv_hbm, w_hbm, out_hbm,
    uv_scr, w_scr, turn_u, turn_v, wave_v, rows_c, rows_s,
    cols_a, cols_b, plain_c, plain_s, edge_r, edge_i, image, in_sem, out_sem,
):
    f32, i32, bf16 = jnp.float32, jnp.int32, jnp.bfloat16
    loads = [pltpu.make_async_copy(uv_hbm, uv_scr, in_sem.at[0]), pltpu.make_async_copy(w_hbm, w_scr, in_sem.at[1])]
    for load in loads:
        load.start()
    for load in loads:
        load.wait()
    low = lax.broadcasted_iota(i32, (LOW, LANES), 0)
    step = lax.broadcasted_iota(i32, (SUB, LANES), 0) + 1

    def row_tables(g):
        u = uv_scr[0, pl.ds(g, 1), :]
        v = uv_scr[1, pl.ds(g, 1), :]
        lc, ls = circle(u * (2 * low + 1 + HALF))
        hc, hs = circle(u * (2 * LOW * step))
        turn_u[0] = hc
        turn_u[1] = hs

        def put(block, c, s):
            at = slice((block + 8) * LOW, (block + 9) * LOW)
            rows_c[g, at, :] = c.astype(bf16)
            rows_s[g, at, :] = s.astype(bf16)

        put(0, lc, ls)
        for h in range(1, 9):
            bc, bs = turn_u[0, h - 1 : h, :], turn_u[1, h - 1 : h, :]
            cc, ss, cs, sc = lc * bc, ls * bs, lc * bs, ls * bc
            put(-h, cc + ss, sc - cs)
            if h < 8:
                put(h, cc - ss, sc + cs)
        lc, ls = circle(v * (2 * low))
        wave_v[0, g] = lc
        wave_v[1, g] = ls
        hc, hs = circle(v * (2 * LOW * step))
        turn_v[0, g] = hc
        turn_v[1, g] = hs

    def prepare(n, carry):
        row_tables(n)
        return carry

    lax.fori_loop(0, GROUPS, prepare, 0)

    lowf = low.astype(f32)

    def turned(g, h, real, imag):
        bc, bs = turn_v[0, g, h - 1 : h, :], turn_v[1, g, h - 1 : h, :]
        rc, ix, rs, ic = real * bc, imag * bs, real * bs, imag * bc
        return {h: (rc - ix, ic + rs), -h: (rc + ix, ic - rs)}

    def weighted(g, f, lc, ls):
        w_r, w_i = w_scr[2 * f, pl.ds(g, 1), :], w_scr[2 * f + 1, pl.ds(g, 1), :]
        return w_r * lc - w_i * ls, w_r * ls + w_i * lc

    def columns(g, blocks):
        lc, ls = wave_v[0, g], wave_v[1, g]
        z_r, z_i = weighted(g, 4, lc, ls)
        plain = {0: (lc, ls)}
        own = {0: (z_r, z_i)}
        for h in sorted({abs(b) for b in blocks} - {0}):
            plain.update(turned(g, h, lc, ls))
            own.update(turned(g, h, z_r, z_i))
        for f, side in ((3, [b for b in blocks if b < -6]), (5, [b for b in blocks if b > 5])):
            if side:
                s_r, s_i = weighted(g, f, lc, ls)
                d_r, d_i = z_r - s_r, z_i - s_i
            for b in side:
                start = (b + 8) * LOW
                if b < 0:
                    taper = (lowf + (start + M + 0.5)) * (1 / (2 * M))
                else:
                    taper = (C + M - 0.5 - start - lowf) * (1 / (2 * M))
                own[b] = turned(g, abs(b), s_r + taper * d_r, s_i + taper * d_i)[b]
        for n, b in enumerate(blocks):
            at = slice(n * LOW, (n + 1) * LOW)
            for refs, values in (((cols_a, cols_b), own[b]), ((plain_c, plain_s), plain[b])):
                refs[0][g, at, :] = values[0].astype(bf16)
                refs[1][g, at, :] = values[1].astype(bf16)

    def edges(g, side):
        u = uv_scr[0, pl.ds(g, 1), :]
        for half in range(M // LOW):
            c, s = edge_wave(g, u, half)
            for f, sign, at in ((side, -1.0, half * LOW), (6 + side, 1.0, M + half * LOW)):
                w_r, w_i = w_scr[2 * f, pl.ds(g, 1), :], w_scr[2 * f + 1, pl.ds(g, 1), :]
                if sign > 0:
                    real, minus = w_r * c - w_i * s, w_r * s + w_i * c
                else:
                    real, minus = w_r * c + w_i * s, w_i * c - w_r * s
                edge_r[side, g, at : at + LOW, :] = real.astype(bf16)
                edge_i[side, g, at : at + LOW, :] = (-minus).astype(bf16)

    def edge_wave(g, u, half):
        return circle(u * (2 * low + 1 + 2 * (EDGE + half * LOW)))

    def inner(g, carry):
        columns(g, INNER)
        edges(g, 1)
        return carry

    lax.fori_loop(0, GROUPS, inner, 0)

    def whole(ref, at=None):
        return jnp.concatenate([ref[g] if at is None else ref[at, g] for g in range(GROUPS)], 1)

    def times(rows, cols):
        return lax.dot_general(rows, cols, (((1,), (1,)), ((), ())), preferred_element_type=f32)

    d = lax.broadcasted_iota(i32, (M, 1), 0).astype(f32)
    t_own = (2 * M - 0.5 - d) * (1 / (2 * M))
    t_next = (d + 0.5) * (1 / (2 * M))
    flip = SUB - 1 - lax.broadcasted_iota(i32, (SUB, LANES), 0)

    def stitch(even, odd, above, below, starts):
        down = even - odd
        up = even + odd
        low_edge = down[EDGE:] * t_own + below * t_next
        high_edge = up[EDGE:] * t_own + above * t_next
        for k, start in enumerate(starts):
            at = slice(k * LANES, (k + 1) * LANES)
            to = slice(start, start + LANES)
            image[HALF : R - M, to] = down[:EDGE, at]
            image[R - M :, to] = low_edge[:, at]
            for i in range(HALF // SUB):
                tile = up[i * SUB : (i + 1) * SUB, at] if i < EDGE // SUB else high_edge[i * SUB - EDGE : (i + 1) * SUB - EDGE, at]
                tile = jnp.take_along_axis(tile, flip, axis=0, mode="promise_in_bounds")
                image[HALF - (i + 1) * SUB : HALF - i * SUB, to] = tile
        return [
            pltpu.make_async_copy(image.at[:, pl.ds(start, width)], out_hbm.at[:, pl.ds(start, width)], out_sem.at[start // LANES])
            for start, width in ([(starts[0], WIDE)] if starts[1] == starts[0] + LANES else [(s, LANES) for s in starts])
        ]

    even = times(whole(rows_c), whole(cols_a))
    odd = times(whole(rows_s), whole(cols_b))
    strip = times(whole(edge_r, 1), whole(plain_c)) + times(whole(edge_i, 1), whole(plain_s))
    out = stitch(even, odd, strip[:M], strip[M:], (LANES, 2 * LANES))
    for copy in out:
        copy.start()

    def outer(g, carry):
        columns(g, OUTER)
        edges(g, 0)
        edges(g, 2)
        return carry

    lax.fori_loop(0, GROUPS, outer, 0)

    column = lax.broadcasted_iota(i32, (1, WIDE), 1)
    column = jnp.where(column < LANES, column, column + C - WIDE).astype(f32)
    t_mid = jnp.minimum(jnp.minimum((column + (M + 0.5)) * (1 / (2 * M)), (C + M - 0.5 - column) * (1 / (2 * M))), 1.0)
    t_left = jnp.maximum(M - 0.5 - column, 0.0) * (1 / (2 * M))
    t_right = jnp.maximum(column - (C - M - 0.5), 0.0) * (1 / (2 * M))
    even = times(whole(rows_c), whole(cols_a))
    odd = times(whole(rows_s), whole(cols_b))
    strip = jnp.zeros((2 * M, WIDE), f32)
    for side, taper in ((0, t_left), (1, t_mid), (2, t_right)):
        strip = strip + (times(whole(edge_r, side), whole(plain_c)) + times(whole(edge_i, side), whole(plain_s))) * taper
    last = stitch(even, odd, strip[:M], strip[M:], (0, C - LANES))
    for copy in last:
        copy.start()
    for copy in out + last:
        copy.wait()


def image_of(uv, w):
    anywhere = pl.BlockSpec(memory_space=pl.ANY)
    f32, bf16 = jnp.float32, jnp.bfloat16
    return pl.pallas_call(
        image_kernel,
        out_shape=jax.ShapeDtypeStruct((R, C), f32),
        in_specs=[anywhere] * 2,
        out_specs=anywhere,
        scratch_shapes=[
            pltpu.VMEM((2, SUB, LANES), jnp.int32),
            pltpu.VMEM((18, SUB, LANES), f32),
            pltpu.VMEM((2, SUB, LANES), f32),
            pltpu.VMEM((2, GROUPS, SUB, LANES), f32),
            pltpu.VMEM((2, GROUPS, LOW, LANES), f32),
            pltpu.VMEM((GROUPS, HALF, LANES), bf16),
            pltpu.VMEM((GROUPS, HALF, LANES), bf16),
            pltpu.VMEM((GROUPS, WIDE, LANES), bf16),
            pltpu.VMEM((GROUPS, WIDE, LANES), bf16),
            pltpu.VMEM((GROUPS, WIDE, LANES), bf16),
            pltpu.VMEM((GROUPS, WIDE, LANES), bf16),
            pltpu.VMEM((3, GROUPS, 2 * M, LANES), bf16),
            pltpu.VMEM((3, GROUPS, 2 * M, LANES), bf16),
            pltpu.VMEM((R, C), f32),
            pltpu.SemaphoreType.DMA((2,)),
            pltpu.SemaphoreType.DMA((4,)),
        ],
        compiler_params=pltpu.CompilerParams(vmem_limit_bytes=56 * 1024 * 1024),
        name="image",
    )(uv, w)


def shards(vis, station_pairs, visibility_time_slot, station_u_cells, station_v_cells, facet_station_gains, holder_device_order):
    gains = facet_station_gains.reshape(2, GAIN_ROWS, LANES).transpose(1, 0, 2).reshape(2 * GAIN_ROWS, LANES)
    uv, w = exchange(
        holder_device_order, vis, station_pairs, visibility_time_slot.reshape(1, BLOCK),
        station_u_cells.reshape(4, LANES), station_v_cells.reshape(4, LANES), gains,
    )
    return image_of(uv, w)


def solution(mesh):
    return jax.shard_map(
        shards,
        mesh=mesh,
        in_specs=(
            P(None, ("frow", "fcol")),
            P(None, ("frow", "fcol")),
            P(("frow", "fcol")),
            P(),
            P(),
            P("frow", "fcol", None, None),
            P(),
        ),
        out_specs=P("frow", "fcol"),
        check_vma=False,
    )
```

```python
import math

import jax
import jax.numpy as jnp
from jax import lax
from jax.experimental import pallas as pl
from jax.experimental.pallas import tpu as pltpu
from jax.sharding import PartitionSpec as P

R = 1024
C = 512
M = 64
NT = 16
NBLK = 4
BLOCK = 256
K = NBLK * BLOCK
N_FROW = 16
N_FCOL = 32
LANES = 128
SUB = 8
GROUPS = K // LANES
SIZE = R * N_FROW
PLANE = 32
DEPTH = 16
PIECES = 10
GAIN_ROWS = 64
MESH = pl.DeviceIdType.MESH
AROUND = [(dr, dc) for dr in (-1, 0, 1) for dc in (-1, 0, 1) if (dr, dc) != (0, 0)]


def place(dr, dc):
    return (1 + dr) * 3 + 1 + dc


def circle(m):
    m = m & (2 * SIZE - 1)
    quarter = (m + SIZE // 4) >> 13
    x = (m - (quarter << 13)).astype(jnp.float32) * (math.pi / SIZE)
    x2 = x * x
    s = x * (1.0 + x2 * (-1 / 6 + x2 * (1 / 120 + x2 * (-1 / 5040 + x2 * (1 / 362880)))))
    c = 1.0 + x2 * (-1 / 2 + x2 * (1 / 24 + x2 * (-1 / 720 + x2 * (1 / 40320))))
    odd = (quarter & 1) == 1
    cos = jnp.where(odd, s, c)
    sin = jnp.where(odd, c, s)
    cos = jnp.where(((quarter + 1) & 2) == 2, -cos, cos)
    sin = jnp.where((quarter & 2) == 2, -sin, sin)
    return cos, sin


def take_lanes(row, index):
    return jnp.take_along_axis(row, index, axis=1, mode="promise_in_bounds")


HALF = R // 2
LOW = 32
WIDE = 256
EDGE = HALF - M
INNER = tuple(range(-4, 4))
MARGIN = (-8, -7, 6, 7)
OUTER = tuple(range(-8, -4)) + tuple(range(4, 8))


def exchange_kernel(
    order_hbm, vis_hbm, pairs_hbm, slot_hbm, ucell_hbm, vcell_hbm, gain_hbm,
    w_ref, wave_v, turn_v, rim_wave, rows_c, rows_s, cols_a, cols_b, plain_c, plain_s, centre, rim,
    order, vis, pairs, slot, ucell, vcell, gain, pay, raw, part, line, done, w_own, w_all, uv_ref, turn_u,
    in_sem, send1, recv1, send2, recv2, send3, recv3, send_w, recv_w,
):
    fr, fc = lax.axis_index("frow"), lax.axis_index("fcol")
    f32, i32, bf16 = jnp.float32, jnp.int32, jnp.bfloat16
    z_lo, y = lax.div(fr, 4), lax.rem(fr, 4)
    z_hi, xc = lax.div(fc, 8), lax.rem(fc, 8)
    me = y * 8 + xc
    my_z = z_hi * 4 + z_lo
    mine = lax.div(me, 3)
    reduces = jnp.logical_and(lax.rem(me, 3) == 0, mine < PIECES)
    plane_row, plane_col = z_lo * 4, z_hi * 8

    def in_plane(s):
        return (plane_row + s // 8, plane_col + s % 8)

    def in_line(z):
        return ((z % 4) * 4 + y, (z // 4) * 8 + xc)

    def inside(dr, dc):
        row, col = fr + dr, fc + dc
        return (row >= 0) & (row < N_FROW) & (col >= 0) & (col < N_FCOL)

    barrier = pltpu.get_barrier_semaphore()

    def greet(device):
        pl.semaphore_signal(barrier, inc=1, device_id=device, device_id_type=MESH)

    @pl.when(reduces)
    def _():
        for z in range(DEPTH):
            @pl.when(my_z != z)
            def _():
                greet(in_line(z))

        for s in range(PLANE):
            @pl.when(me != s)
            def _():
                greet(in_plane(s))

    @pl.when(jnp.logical_not(reduces))
    def _():
        for j in range(PIECES):
            greet(in_plane(3 * j))

    count = jnp.where(reduces, PLANE - 1 + DEPTH - 1, PIECES)
    for dr, dc in AROUND:
        count = count + inside(dr, dc).astype(i32)

        @pl.when(inside(dr, dc))
        def _():
            greet((fr + dr, fc + dc))

    loads = ((vis_hbm, vis), (pairs_hbm, pairs), (slot_hbm, slot), (order_hbm, order), (ucell_hbm, ucell), (vcell_hbm, vcell), (gain_hbm, gain))
    loads = [pltpu.make_async_copy(a, b, in_sem.at[n]) for n, (a, b) in enumerate(loads)]
    for load in loads:
        load.start()
    for dr, dc in AROUND:
        @pl.when(jnp.logical_not(inside(dr, dc)))
        def _():
            w_all[place(dr, dc)] = jnp.zeros((2, SUB, LANES), f32)

    for load in loads:
        load.wait()
    for half in range(2):
        cols = slice(half * LANES, (half + 1) * LANES)
        pay[half] = vis[0:1, cols]
        pay[2 + half] = vis[1:2, cols]
        pay[4 + half] = pairs[0:1, cols].astype(f32)
        pay[6 + half] = pairs[1:2, cols].astype(f32)
        pay[8 + half] = slot[0:1, cols].astype(f32)

    pl.semaphore_wait(barrier, count)

    def piece_copy(j):
        return pltpu.make_async_remote_copy(
            src_ref=pay.at[j], dst_ref=raw.at[me], send_sem=send1.at[j], recv_sem=recv1,
            device_id=in_plane(3 * j), device_id_type=MESH,
        )

    def line_copy(z):
        return pltpu.make_async_remote_copy(
            src_ref=part, dst_ref=line.at[my_z], send_sem=send2.at[z], recv_sem=recv2,
            device_id=in_line(z), device_id_type=MESH,
        )

    def done_copy(s):
        return pltpu.make_async_remote_copy(
            src_ref=done.at[mine], dst_ref=done.at[mine], send_sem=send3.at[s], recv_sem=recv3,
            device_id=in_plane(s), device_id_type=MESH,
        )

    def weight_copy(dr, dc):
        return pltpu.make_async_remote_copy(
            src_ref=w_own, dst_ref=w_all.at[place(-dr, -dc)],
            send_sem=send_w.at[place(dr, dc)], recv_sem=recv_w.at[place(-dr, -dc)],
            device_id=(fr + dr, fc + dc), device_id_type=MESH,
        )

    def landed(ref, slots, sem):
        view = ref.at[pl.ds(0, slots)]
        pltpu.make_async_copy(view, view, sem).wait()

    for j in range(PIECES):
        @pl.when(me != 3 * j)
        def _():
            piece_copy(j).start()

    @pl.when(reduces)
    def _():
        raw[me] = pay[mine]
        s = lax.broadcasted_iota(i32, (PLANE, 1, LANES), 0)
        holder = (plane_row + (s >> 3)) * N_FCOL + plane_col + (s & 7)
        landed(raw, PLANE - 1, recv1)
        values = raw[...]
        for b in range(NBLK):
            part[b : b + 1, :] = jnp.sum(jnp.where(holder == order[b], values, 0.0), axis=0)
        for z in range(DEPTH):
            @pl.when(my_z != z)
            def _():
                line_copy(z).start()

        line[my_z] = part[...]
        landed(line, DEPTH - 1, recv2)
        done[mine] = jnp.sum(line[...], axis=0)
        for s in range(PLANE):
            @pl.when(me != s)
            def _():
                done_copy(s).start()

        landed(done, PIECES - 1, recv3)

    @pl.when(jnp.logical_not(reduces))
    def _():
        landed(done, PIECES, recv3)

    def value(v):
        return jnp.concatenate([done[2 * v], done[2 * v + 1]], 0)

    s1, s2, t = value(2).astype(i32), value(3).astype(i32), value(4).astype(i32)
    first, second = s1 * NT + t, s2 * NT + t

    def pick(part, index):
        lane, row = index & 127, index >> 7
        bits = [(row & (1 << b)) != 0 for b in range(6)]
        stack = []
        for n in range(GAIN_ROWS):
            values = jnp.broadcast_to(gain[2 * n + part : 2 * n + part + 1, :], (SUB, LANES))
            found, level = take_lanes(values, lane), 0
            while stack and stack[-1][0] == level:
                found = jnp.where(bits[level], found, stack.pop()[1])
                level += 1
            stack.append((level, found))
        return stack[0][1]

    scale = 0.5 / math.sqrt(K)
    v_r, v_i = value(0), value(1)
    g1r, g1i = pick(0, first), pick(1, first)
    g2r, g2i = pick(0, second), pick(1, second)
    real_gain = g1r * g2r + g1i * g2i
    imag_gain = g1i * g2r - g1r * g2i
    w_own[0] = scale * (v_r * real_gain - v_i * imag_gain)
    w_own[1] = scale * (v_r * imag_gain + v_i * real_gain)
    for dr, dc in AROUND:
        @pl.when(inside(dr, dc))
        def _():
            weight_copy(dr, dc).start()

    def station(ref):
        total = jnp.zeros((SUB, LANES), i32)
        for row in range(4):
            cells = jnp.broadcast_to(ref[row : row + 1, :], (SUB, LANES))
            one = take_lanes(cells, s1 & 127)
            two = take_lanes(cells, s2 & 127)
            total = total + jnp.where((s1 >> 7) == row, one, 0) - jnp.where((s2 >> 7) == row, two, 0)
        return total

    u, v = station(ucell), station(vcell)
    uv_ref[0] = u
    uv_ref[1] = v
    mid_c, mid_s = circle(u * (fr * (2 * R) + R - 1) + v * (2 * (fc * C + C // 2)))

    def turn(place_of, w_r, w_i):
        w_ref[2 * place_of] = w_r * mid_c - w_i * mid_s
        w_ref[2 * place_of + 1] = w_r * mid_s + w_i * mid_c

    turn(4, w_own[0], w_own[1])

    low = lax.broadcasted_iota(i32, (LOW, LANES), 0)
    step = lax.broadcasted_iota(i32, (SUB, LANES), 0) + 1

    def row_tables(g):
        u = uv_ref[0, pl.ds(g, 1), :]
        v = uv_ref[1, pl.ds(g, 1), :]
        lc, ls = circle(u * (2 * low + 1 + HALF))
        hc, hs = circle(u * (2 * LOW * step))
        turn_u[0] = hc
        turn_u[1] = hs

        def put(block, c, s):
            at = slice((block + 8) * LOW, (block + 9) * LOW)
            rows_c[g, at, :] = c.astype(bf16)
            rows_s[g, at, :] = s.astype(bf16)
            if block >= 6:
                rim_wave[0, g, (block - 6) * LOW : (block - 5) * LOW, :] = c
                rim_wave[1, g, (block - 6) * LOW : (block - 5) * LOW, :] = s

        put(0, lc, ls)
        for h in range(1, 9):
            bc, bs = turn_u[0, h - 1 : h, :], turn_u[1, h - 1 : h, :]
            cc, ss, cs, sc = lc * bc, ls * bs, lc * bs, ls * bc
            put(-h, cc + ss, sc - cs)
            if h < 8:
                put(h, cc - ss, sc + cs)
        lc, ls = circle(v * (2 * low))
        wave_v[0, g] = lc
        wave_v[1, g] = ls
        hc, hs = circle(v * (2 * LOW * step))
        turn_v[0, g] = hc
        turn_v[1, g] = hs

    def prepare(n, carry):
        row_tables(n)
        return carry

    lax.fori_loop(0, GROUPS, prepare, 0)

    lowf = low.astype(f32)

    def turned(g, h, real, imag):
        bc, bs = turn_v[0, g, h - 1 : h, :], turn_v[1, g, h - 1 : h, :]
        rc, ix, rs, ic = real * bc, imag * bs, real * bs, imag * bc
        return {h: (rc - ix, ic + rs), -h: (rc + ix, ic - rs)}

    def weighted(g, f, lc, ls):
        w_r, w_i = w_ref[2 * f, pl.ds(g, 1), :], w_ref[2 * f + 1, pl.ds(g, 1), :]
        return w_r * lc - w_i * ls, w_r * ls + w_i * lc

    def keep(g, spot, block, own, plain):
        at = slice(block * LOW, (block + 1) * LOW)
        if own is not None:
            cols_a[spot, g, at, :] = own[0].astype(bf16)
            cols_b[spot, g, at, :] = own[1].astype(bf16)
        if plain is not None:
            plain_c[spot, g, at, :] = plain[0].astype(bf16)
            plain_s[spot, g, at, :] = plain[1].astype(bf16)

    def columns(g, spot):
        blocks = (INNER, OUTER)[spot]
        lc, ls = wave_v[0, g], wave_v[1, g]
        z_r, z_i = weighted(g, 4, lc, ls)
        plain = {0: (lc, ls)}
        own = {0: (z_r, z_i)}
        for h in sorted({abs(b) for b in blocks} - {0}):
            plain.update(turned(g, h, lc, ls))
            if h < 7:
                own.update(turned(g, h, z_r, z_i))
        for n, b in enumerate(blocks):
            keep(g, spot, n, own[b] if -7 < b < 6 else None, plain[b])

    def inner(g, carry):
        columns(g, 0)
        return carry

    lax.fori_loop(0, GROUPS, inner, 0)

    def whole(ref, at=None):
        return jnp.concatenate([ref[g] if at is None else ref[at, g] for g in range(GROUPS)], 1)

    def times(rows, cols):
        return lax.dot_general(rows, cols, (((1,), (1,)), ((), ())), preferred_element_type=f32)

    flip = SUB - 1 - lax.broadcasted_iota(i32, (SUB, LANES), 0)

    def lay(even, odd):
        down = even - odd
        up = even + odd
        rim[0] = up[EDGE:]
        rim[1] = down[EDGE:]
        centre[EDGE:, :] = down[:EDGE]
        for i in range(EDGE // SUB):
            for k in range(WIDE // LANES):
                at = slice(k * LANES, (k + 1) * LANES)
                tile = jnp.take_along_axis(up[i * SUB : (i + 1) * SUB, at], flip, axis=0, mode="promise_in_bounds")
                centre[EDGE - (i + 1) * SUB : EDGE - i * SUB, at] = tile

    lay(times(whole(rows_c), whole(cols_a, 0)), times(whole(rows_s), whole(cols_b, 0)))
    for g in range(GROUPS):
        columns(g, 1)

    for j in range(PIECES):
        @pl.when(me != 3 * j)
        def _():
            piece_copy(j).wait_send()

    @pl.when(reduces)
    def _():
        for z in range(DEPTH):
            @pl.when(my_z != z)
            def _():
                line_copy(z).wait_send()

        for s in range(PLANE):
            @pl.when(me != s)
            def _():
                done_copy(s).wait_send()

    for dr, dc in AROUND:
        @pl.when(inside(dr, dc))
        def _():
            weight_copy(dr, dc).wait_send()
            slot_of = w_all.at[place(dr, dc)]
            pltpu.make_async_copy(slot_of, slot_of, recv_w.at[place(dr, dc)]).wait()

    for dr, dc in AROUND:
        turn(place(dr, dc), w_all[place(dr, dc), 0], w_all[place(dr, dc), 1])


def image_kernel(
    w_ref, wave_v, turn_v, rim_wave, rows_c, rows_s, cols_a, cols_b, plain_c, plain_s, centre, rim, out_hbm,
    edge_a, edge_b, edge_r, edge_i, image, out_sem,
):
    f32, i32, bf16 = jnp.float32, jnp.int32, jnp.bfloat16

    def store(n, source, rows, cols):
        copy = pltpu.make_async_copy(source, out_hbm.at[pl.ds(*rows), pl.ds(*cols)], out_sem.at[n])
        copy.start()
        return copy

    stores = [store(0, centre, (M, 2 * EDGE), (LANES, WIDE))]
    low = lax.broadcasted_iota(i32, (LOW, LANES), 0)
    lowf = low.astype(f32)

    def turned(g, h, real, imag):
        bc, bs = turn_v[0, g, h - 1 : h, :], turn_v[1, g, h - 1 : h, :]
        rc, ix, rs, ic = real * bc, imag * bs, real * bs, imag * bc
        return {h: (rc - ix, ic + rs), -h: (rc + ix, ic - rs)}

    def weighted(g, f, lc, ls):
        w_r, w_i = w_ref[2 * f, pl.ds(g, 1), :], w_ref[2 * f + 1, pl.ds(g, 1), :]
        return w_r * lc - w_i * ls, w_r * ls + w_i * lc

    def keep(g, block, own):
        at = slice(block * LOW, (block + 1) * LOW)
        edge_a[g, at, :] = own[0].astype(bf16)
        edge_b[g, at, :] = own[1].astype(bf16)

    def shared(g):
        lc, ls = wave_v[0, g], wave_v[1, g]
        z_r, z_i = weighted(g, 4, lc, ls)
        for f, side in ((3, (-8, -7)), (5, (6, 7))):
            s_r, s_i = weighted(g, f, lc, ls)
            d_r, d_i = z_r - s_r, z_i - s_i
            for b in side:
                start = (b + 8) * LOW
                if b < 0:
                    taper = (lowf + (start + M + 0.5)) * (1 / (2 * M))
                else:
                    taper = (C + M - 0.5 - start - lowf) * (1 / (2 * M))
                keep(g, MARGIN.index(b), turned(g, abs(b), s_r + taper * d_r, s_i + taper * d_i)[b])

    def edges(g, side):
        for half in range(M // LOW):
            at_half = slice(half * LOW, (half + 1) * LOW)
            c, s = rim_wave[0, g, at_half, :], rim_wave[1, g, at_half, :]
            for f, sign, at in ((side, -1.0, half * LOW), (6 + side, 1.0, M + half * LOW)):
                w_r, w_i = w_ref[2 * f, pl.ds(g, 1), :], w_ref[2 * f + 1, pl.ds(g, 1), :]
                if sign > 0:
                    real, minus = w_r * c - w_i * s, w_r * s + w_i * c
                else:
                    real, minus = w_r * c + w_i * s, w_i * c - w_r * s
                edge_r[side, g, at : at + LOW, :] = real.astype(bf16)
                edge_i[side, g, at : at + LOW, :] = (-minus).astype(bf16)

    def whole(ref, at=None):
        return jnp.concatenate([ref[g] if at is None else ref[at, g] for g in range(GROUPS)], 1)

    def times(rows, cols):
        return lax.dot_general(rows, cols, (((1,), (1,)), ((), ())), preferred_element_type=f32)

    d = lax.broadcasted_iota(i32, (M, 1), 0).astype(f32)
    t_own = (2 * M - 0.5 - d) * (1 / (2 * M))
    t_next = (d + 0.5) * (1 / (2 * M))
    flip = SUB - 1 - lax.broadcasted_iota(i32, (SUB, LANES), 0)

    def lay(down, up, start):
        to = slice(start, start + LANES)
        image[HALF : R - M, to] = down[:EDGE]
        for i in range(EDGE // SUB):
            tile = jnp.take_along_axis(up[i * SUB : (i + 1) * SUB], flip, axis=0, mode="promise_in_bounds")
            image[HALF - (i + 1) * SUB : HALF - i * SUB, to] = tile

    def seam(up, down, strip, start):
        to = slice(start, start + LANES)
        top = up * t_own + strip[:M] * t_next
        image[R - M :, to] = down * t_own + strip[M:] * t_next
        for i in range(M // SUB):
            tile = jnp.take_along_axis(top[i * SUB : (i + 1) * SUB], flip, axis=0, mode="promise_in_bounds")
            image[M - (i + 1) * SUB : M - i * SUB, to] = tile

    def rest(g, carry):
        shared(g)
        for side in range(3):
            edges(g, side)
        return carry

    lax.fori_loop(0, GROUPS, rest, 0)

    column = lax.broadcasted_iota(i32, (1, WIDE), 1)
    column = jnp.where(column < LANES, column, column + C - WIDE).astype(f32)
    t_mid = jnp.minimum(jnp.minimum((column + (M + 0.5)) * (1 / (2 * M)), (C + M - 0.5 - column) * (1 / (2 * M))), 1.0)
    t_left = jnp.maximum(M - 0.5 - column, 0.0) * (1 / (2 * M))
    t_right = jnp.maximum(column - (C - M - 0.5), 0.0) * (1 / (2 * M))

    def strip_of(side, spot):
        return times(whole(edge_r, side), whole(plain_c, spot)) + times(whole(edge_i, side), whole(plain_s, spot))

    def outer_cols(inner_ref, edge_ref):
        parts = []
        for g in range(GROUPS):
            own = inner_ref[1, g]
            parts.append(jnp.concatenate([edge_ref[g, : 2 * LOW], own[2 * LOW : 6 * LOW], edge_ref[g, 2 * LOW :]], 0))
        return jnp.concatenate(parts, 1)

    even = times(whole(rows_c), outer_cols(cols_a, edge_a))
    odd = times(whole(rows_s), outer_cols(cols_b, edge_b))
    down, up = even - odd, even + odd
    for k, start in ((0, 0), (1, C - LANES)):
        at = slice(k * LANES, (k + 1) * LANES)
        lay(down[:EDGE, at], up[:EDGE, at], start)
        stores.append(store(1 + k, image.at[pl.ds(M, 2 * EDGE), pl.ds(start, LANES)], (M, 2 * EDGE), (start, LANES)))
    strip = strip_of(1, 0)
    for k in range(2):
        at = slice(k * LANES, (k + 1) * LANES)
        seam(rim[0, :, at], rim[1, :, at], strip[:, at], (k + 1) * LANES)
    strip = strip_of(0, 1) * t_left + strip_of(1, 1) * t_mid + strip_of(2, 1) * t_right
    for k, start in ((0, 0), (1, C - LANES)):
        at = slice(k * LANES, (k + 1) * LANES)
        seam(up[EDGE:, at], down[EDGE:, at], strip[:, at], start)
    for n, row in ((3, 0), (4, R - M)):
        stores.append(store(n, image.at[pl.ds(row, M)], (row, M), (0, C)))
    for copy in stores:
        copy.wait()


def tile_of(order, vis, pairs, slot, ucell, vcell, gain):
    dma, vmem = pltpu.SemaphoreType.DMA, pltpu.VMEM
    f32, i32, bf16 = jnp.float32, jnp.int32, jnp.bfloat16
    inside = pl.BlockSpec(memory_space=pltpu.VMEM)
    kept = (
        vmem((18, SUB, LANES), f32),
        vmem((2, GROUPS, LOW, LANES), f32),
        vmem((2, GROUPS, SUB, LANES), f32),
        vmem((2, GROUPS, M, LANES), f32),
        vmem((GROUPS, HALF, LANES), bf16),
        vmem((GROUPS, HALF, LANES), bf16),
        vmem((2, GROUPS, WIDE, LANES), bf16),
        vmem((2, GROUPS, WIDE, LANES), bf16),
        vmem((2, GROUPS, WIDE, LANES), bf16),
        vmem((2, GROUPS, WIDE, LANES), bf16),
        vmem((2 * EDGE, WIDE), f32),
        vmem((2, M, WIDE), f32),
    )
    tables = pl.pallas_call(
        exchange_kernel,
        out_shape=kept,
        in_specs=[pl.BlockSpec(memory_space=pltpu.HBM)] * 7,
        out_specs=(inside,) * len(kept),
        scratch_shapes=[
            pltpu.SMEM((N_FROW * N_FCOL,), i32),
            vmem((2, BLOCK), f32),
            vmem((2, BLOCK), i32),
            vmem((1, BLOCK), i32),
            vmem((4, LANES), i32),
            vmem((4, LANES), i32),
            vmem((2 * GAIN_ROWS, LANES), f32),
            vmem((PIECES, 1, LANES), f32),
            vmem((PLANE, 1, LANES), f32),
            vmem((NBLK, LANES), f32),
            vmem((DEPTH, NBLK, LANES), f32),
            vmem((PIECES, NBLK, LANES), f32),
            vmem((2, SUB, LANES), f32),
            vmem((9, 2, SUB, LANES), f32),
            vmem((2, SUB, LANES), i32),
            vmem((2, SUB, LANES), f32),
            dma((7,)), dma((PIECES,)), dma, dma((DEPTH,)), dma, dma((PLANE,)), dma, dma((9,)), dma((9,)),
        ],
        compiler_params=pltpu.CompilerParams(collective_id=0, has_side_effects=True, vmem_limit_bytes=24 * 1024 * 1024),
        name="exchange",
    )(*[pltpu.with_memory_space_constraint(x, pltpu.HBM) for x in (order, vis, pairs, slot, ucell, vcell, gain)])
    return pl.pallas_call(
        image_kernel,
        out_shape=jax.ShapeDtypeStruct((R, C), f32),
        in_specs=[inside] * len(kept),
        out_specs=pl.BlockSpec(memory_space=pl.ANY),
        scratch_shapes=[
            vmem((GROUPS, 2 * M, LANES), bf16),
            vmem((GROUPS, 2 * M, LANES), bf16),
            vmem((3, GROUPS, 2 * M, LANES), bf16),
            vmem((3, GROUPS, 2 * M, LANES), bf16),
            vmem((R, C), f32),
            dma((5,)),
        ],
        compiler_params=pltpu.CompilerParams(vmem_limit_bytes=24 * 1024 * 1024),
        name="image",
    )(*tables)


def shards(vis, station_pairs, visibility_time_slot, station_u_cells, station_v_cells, facet_station_gains, holder_device_order):
    gains = facet_station_gains.reshape(2, GAIN_ROWS, LANES).transpose(1, 0, 2).reshape(2 * GAIN_ROWS, LANES)
    return tile_of(
        holder_device_order, vis, station_pairs, visibility_time_slot.reshape(1, BLOCK),
        station_u_cells.reshape(4, LANES), station_v_cells.reshape(4, LANES), gains,
    )


def solution(mesh):
    return jax.shard_map(
        shards,
        mesh=mesh,
        in_specs=(
            P(None, ("frow", "fcol")),
            P(None, ("frow", "fcol")),
            P(("frow", "fcol")),
            P(),
            P(),
            P("frow", "fcol", None, None),
            P(),
        ),
        out_specs=P("frow", "fcol"),
        check_vma=False,
    )
```

```python
import math

import jax
import jax.numpy as jnp
from jax import lax
from jax.experimental import pallas as pl
from jax.experimental.pallas import tpu as pltpu
from jax.sharding import PartitionSpec as P

R = 1024
C = 512
M = 64
NT = 16
NBLK = 4
BLOCK = 256
K = NBLK * BLOCK
N_FROW = 16
N_FCOL = 32
LANES = 128
SUB = 8
GROUPS = K // LANES
SIZE = R * N_FROW
PLANE = 32
DEPTH = 16
PIECES = 10
REDUCERS = tuple(6 * (j // 2) + j % 2 for j in range(PIECES))
PEERS = REDUCERS + tuple(s for s in range(PLANE) if s not in REDUCERS)
GAIN_ROWS = 64
MESH = pl.DeviceIdType.MESH
AROUND = [(dr, dc) for dr in (-1, 0, 1) for dc in (-1, 0, 1) if (dr, dc) != (0, 0)]


def place(dr, dc):
    return (1 + dr) * 3 + 1 + dc


def circle(m):
    m = m & (2 * SIZE - 1)
    quarter = (m + SIZE // 4) >> 13
    x = (m - (quarter << 13)).astype(jnp.float32) * (math.pi / SIZE)
    x2 = x * x
    s = x * (1.0 + x2 * (-1 / 6 + x2 * (1 / 120 + x2 * (-1 / 5040 + x2 * (1 / 362880)))))
    c = 1.0 + x2 * (-1 / 2 + x2 * (1 / 24 + x2 * (-1 / 720 + x2 * (1 / 40320))))
    odd = (quarter & 1) == 1
    cos = jnp.where(odd, s, c)
    sin = jnp.where(odd, c, s)
    cos = jnp.where(((quarter + 1) & 2) == 2, -cos, cos)
    sin = jnp.where((quarter & 2) == 2, -sin, sin)
    return cos, sin


def take_lanes(row, index):
    return jnp.take_along_axis(row, index, axis=1, mode="promise_in_bounds")


HALF = R // 2
LOW = 32
WIDE = 256
EDGE = HALF - M
INNER = tuple(range(-4, 4))
MARGIN = (-8, -7, 6, 7)
OUTER = tuple(range(-8, -4)) + tuple(range(4, 8))


def exchange_kernel(
    order_hbm, vis_hbm, pairs_hbm, slot_hbm, ucell_hbm, vcell_hbm, gain_hbm,
    w_ref, wave_v, turn_v, rim_wave, rows_c, rows_s, cols_a, cols_b, plain_c, plain_s, centre, rim,
    order, vis, pairs, slot, ucell, vcell, gain, pay, raw, part, line, done, w_own, w_all, uv_ref, turn_u, spin,
    in_sem, send1, recv1, send2, recv2, send3, recv3, send_w, recv_w,
):
    fr, fc = lax.axis_index("frow"), lax.axis_index("fcol")
    f32, i32, bf16 = jnp.float32, jnp.int32, jnp.bfloat16
    z_lo, y = lax.div(fr, 4), lax.rem(fr, 4)
    z_hi, xc = lax.div(fc, 8), lax.rem(fc, 8)
    me = y * 8 + xc
    my_z = z_hi * 4 + z_lo
    mine = 2 * lax.div(me, 6) + lax.rem(me, 6)
    reduces = jnp.logical_and(lax.rem(me, 6) < 2, mine < PIECES)
    plane_row, plane_col = z_lo * 4, z_hi * 8

    def in_plane(s):
        return (plane_row + s // 8, plane_col + s % 8)

    def in_line(z):
        return ((z % 4) * 4 + y, (z // 4) * 8 + xc)

    def inside(dr, dc):
        row, col = fr + dr, fc + dc
        return (row >= 0) & (row < N_FROW) & (col >= 0) & (col < N_FCOL)

    loads = ((vis_hbm, vis), (pairs_hbm, pairs), (slot_hbm, slot), (order_hbm, order), (ucell_hbm, ucell), (vcell_hbm, vcell), (gain_hbm, gain))
    loads = [pltpu.make_async_copy(a, b, in_sem.at[n]) for n, (a, b) in enumerate(loads)]
    for load in loads[:4]:
        load.start()
    barrier = pltpu.get_barrier_semaphore()

    def greet(device):
        pl.semaphore_signal(barrier, inc=1, device_id=device, device_id_type=MESH)

    @pl.when(reduces)
    def _():
        for z in range(DEPTH):
            @pl.when(my_z != z)
            def _():
                greet(in_line(z))

        for s in range(PLANE):
            @pl.when(me != s)
            def _():
                greet(in_plane(s))

    @pl.when(jnp.logical_not(reduces))
    def _():
        for j in range(PIECES):
            greet(in_plane(REDUCERS[j]))

    count = jnp.where(reduces, PLANE - 1 + DEPTH - 1, PIECES)
    for dr, dc in AROUND:
        count = count + inside(dr, dc).astype(i32)

        @pl.when(inside(dr, dc))
        def _():
            greet((fr + dr, fc + dc))

    for load in loads[4:]:
        load.start()
    for dr, dc in AROUND:
        @pl.when(jnp.logical_not(inside(dr, dc)))
        def _():
            w_all[place(dr, dc)] = jnp.zeros((2, SUB, LANES), f32)

    for load in loads[:4]:
        load.wait()
    for half in range(2):
        cols = slice(half * LANES, (half + 1) * LANES)
        pay[half] = vis[0:1, cols]
        pay[2 + half] = vis[1:2, cols]
        pay[4 + half] = pairs[0:1, cols].astype(f32)
        pay[6 + half] = pairs[1:2, cols].astype(f32)
        pay[8 + half] = slot[0:1, cols].astype(f32)

    pl.semaphore_wait(barrier, count)

    def piece_copy(j):
        return pltpu.make_async_remote_copy(
            src_ref=pay.at[j], dst_ref=raw.at[me], send_sem=send1.at[j], recv_sem=recv1,
            device_id=in_plane(REDUCERS[j]), device_id_type=MESH,
        )

    def line_copy(z):
        return pltpu.make_async_remote_copy(
            src_ref=part, dst_ref=line.at[my_z], send_sem=send2.at[z], recv_sem=recv2,
            device_id=in_line(z), device_id_type=MESH,
        )

    def done_copy(s):
        return pltpu.make_async_remote_copy(
            src_ref=done.at[mine], dst_ref=done.at[mine], send_sem=send3.at[s], recv_sem=recv3,
            device_id=in_plane(s), device_id_type=MESH,
        )

    def weight_copy(dr, dc):
        return pltpu.make_async_remote_copy(
            src_ref=w_own, dst_ref=w_all.at[place(-dr, -dc)],
            send_sem=send_w.at[place(dr, dc)], recv_sem=recv_w.at[place(-dr, -dc)],
            device_id=(fr + dr, fc + dc), device_id_type=MESH,
        )

    def landed(ref, slots, sem):
        view = ref.at[pl.ds(0, slots)]
        pltpu.make_async_copy(view, view, sem).wait()

    for j in range(PIECES):
        @pl.when(me != REDUCERS[j])
        def _():
            piece_copy(j).start()

    @pl.when(reduces)
    def _():
        raw[me] = pay[mine]
        s = lax.broadcasted_iota(i32, (PLANE, 1, LANES), 0)
        holder = (plane_row + (s >> 3)) * N_FCOL + plane_col + (s & 7)
        landed(raw, PLANE - 1, recv1)
        values = raw[...]
        for b in range(NBLK):
            part[b : b + 1, :] = jnp.sum(jnp.where(holder == order[b], values, 0.0), axis=0)
        for z in range(DEPTH):
            @pl.when(my_z != z)
            def _():
                line_copy(z).start()

        line[my_z] = part[...]
        landed(line, DEPTH - 1, recv2)
        done[mine] = jnp.sum(line[...], axis=0)
        for s in PEERS:
            @pl.when(me != s)
            def _():
                done_copy(s).start()

        landed(done, PIECES - 1, recv3)

    @pl.when(jnp.logical_not(reduces))
    def _():
        landed(done, PIECES, recv3)

    for load in loads[4:]:
        load.wait()

    def value(v):
        return jnp.concatenate([done[2 * v], done[2 * v + 1]], 0)

    s1, s2, t = value(2).astype(i32), value(3).astype(i32), value(4).astype(i32)
    first, second = s1 * NT + t, s2 * NT + t

    def pick(part, index):
        lane, row = index & 127, index >> 7
        bits = [(row & (1 << b)) != 0 for b in range(6)]
        stack = []
        for n in range(GAIN_ROWS):
            values = jnp.broadcast_to(gain[2 * n + part : 2 * n + part + 1, :], (SUB, LANES))
            found, level = take_lanes(values, lane), 0
            while stack and stack[-1][0] == level:
                found = jnp.where(bits[level], found, stack.pop()[1])
                level += 1
            stack.append((level, found))
        return stack[0][1]

    scale = 0.5 / math.sqrt(K)
    v_r, v_i = value(0), value(1)
    g1r, g1i = pick(0, first), pick(1, first)
    g2r, g2i = pick(0, second), pick(1, second)
    real_gain = g1r * g2r + g1i * g2i
    imag_gain = g1i * g2r - g1r * g2i
    w_own[0] = scale * (v_r * real_gain - v_i * imag_gain)
    w_own[1] = scale * (v_r * imag_gain + v_i * real_gain)
    for dr, dc in AROUND:
        @pl.when(inside(dr, dc))
        def _():
            weight_copy(dr, dc).start()

    def station(ref):
        total = jnp.zeros((SUB, LANES), i32)
        for row in range(4):
            cells = jnp.broadcast_to(ref[row : row + 1, :], (SUB, LANES))
            one = take_lanes(cells, s1 & 127)
            two = take_lanes(cells, s2 & 127)
            total = total + jnp.where((s1 >> 7) == row, one, 0) - jnp.where((s2 >> 7) == row, two, 0)
        return total

    u, v = station(ucell), station(vcell)
    uv_ref[0] = u
    uv_ref[1] = v
    mid_c, mid_s = circle(u * (fr * (2 * R) + R - 1) + v * (2 * (fc * C + C // 2)))

    def turn(place_of, w_r, w_i):
        w_ref[2 * place_of] = w_r * mid_c - w_i * mid_s
        w_ref[2 * place_of + 1] = w_r * mid_s + w_i * mid_c

    turn(4, w_own[0], w_own[1])

    low = lax.broadcasted_iota(i32, (LOW, LANES), 0)
    step = lax.broadcasted_iota(i32, (SUB, LANES), 0) + 1

    for n, cells in enumerate((uv_ref[0], uv_ref[1])):
        for i in range(1, LOW // SUB):
            spin[n, i - 1, 0], spin[n, i - 1, 1] = circle(cells * (2 * SUB * i))

    def fan(n, g, c, s):
        cos, sin = [c], [s]
        for i in range(LOW // SUB - 1):
            bc, bs = spin[n, i, 0, pl.ds(g, 1), :], spin[n, i, 1, pl.ds(g, 1), :]
            cos.append(c * bc - s * bs)
            sin.append(s * bc + c * bs)
        return jnp.concatenate(cos, 0), jnp.concatenate(sin, 0)

    def row_tables(g):
        u = uv_ref[0, pl.ds(g, 1), :]
        v = uv_ref[1, pl.ds(g, 1), :]
        lc, ls = fan(0, g, *circle(u * (2 * step - 1 + HALF)))
        hc, hs = circle(u * (2 * LOW * step))
        turn_u[0] = hc
        turn_u[1] = hs

        def put(block, c, s):
            at = slice((block + 8) * LOW, (block + 9) * LOW)
            rows_c[g, at, :] = c.astype(bf16)
            rows_s[g, at, :] = s.astype(bf16)
            if block >= 6:
                rim_wave[0, g, (block - 6) * LOW : (block - 5) * LOW, :] = c
                rim_wave[1, g, (block - 6) * LOW : (block - 5) * LOW, :] = s

        put(0, lc, ls)
        for h in range(1, 9):
            bc, bs = turn_u[0, h - 1 : h, :], turn_u[1, h - 1 : h, :]
            cc, ss, cs, sc = lc * bc, ls * bs, lc * bs, ls * bc
            put(-h, cc + ss, sc - cs)
            if h < 8:
                put(h, cc - ss, sc + cs)
        lc, ls = fan(1, g, *circle(v * (2 * step - 2)))
        wave_v[0, g] = lc
        wave_v[1, g] = ls
        hc, hs = circle(v * (2 * LOW * step))
        turn_v[0, g] = hc
        turn_v[1, g] = hs

    def prepare(n, carry):
        row_tables(n)
        return carry

    lax.fori_loop(0, GROUPS, prepare, 0)

    lowf = low.astype(f32)

    def turned(g, h, real, imag):
        bc, bs = turn_v[0, g, h - 1 : h, :], turn_v[1, g, h - 1 : h, :]
        rc, ix, rs, ic = real * bc, imag * bs, real * bs, imag * bc
        return {h: (rc - ix, ic + rs), -h: (rc + ix, ic - rs)}

    def weighted(g, f, lc, ls):
        w_r, w_i = w_ref[2 * f, pl.ds(g, 1), :], w_ref[2 * f + 1, pl.ds(g, 1), :]
        return w_r * lc - w_i * ls, w_r * ls + w_i * lc

    def keep(g, spot, block, own, plain):
        at = slice(block * LOW, (block + 1) * LOW)
        if own is not None:
            cols_a[spot, g, at, :] = own[0].astype(bf16)
            cols_b[spot, g, at, :] = own[1].astype(bf16)
        if plain is not None:
            plain_c[spot, g, at, :] = plain[0].astype(bf16)
            plain_s[spot, g, at, :] = plain[1].astype(bf16)

    def columns(g, spot):
        blocks = (INNER, OUTER)[spot]
        lc, ls = wave_v[0, g], wave_v[1, g]
        z_r, z_i = weighted(g, 4, lc, ls)
        plain = {0: (lc, ls)}
        own = {0: (z_r, z_i)}
        for h in sorted({abs(b) for b in blocks} - {0}):
            plain.update(turned(g, h, lc, ls))
            if h < 7:
                own.update(turned(g, h, z_r, z_i))
        for n, b in enumerate(blocks):
            keep(g, spot, n, own[b] if -7 < b < 6 else None, plain[b])

    def inner(g, carry):
        columns(g, 0)
        return carry

    lax.fori_loop(0, GROUPS, inner, 0)

    def whole(ref, at=None):
        return jnp.concatenate([ref[g] if at is None else ref[at, g] for g in range(GROUPS)], 1)

    def times(rows, cols):
        return lax.dot_general(rows, cols, (((1,), (1,)), ((), ())), preferred_element_type=f32)

    flip = SUB - 1 - lax.broadcasted_iota(i32, (SUB, LANES), 0)

    def lay(even, odd):
        down = even - odd
        up = even + odd
        rim[0] = up[EDGE:]
        rim[1] = down[EDGE:]
        centre[EDGE:, :] = down[:EDGE]
        for i in range(EDGE // SUB):
            for k in range(WIDE // LANES):
                at = slice(k * LANES, (k + 1) * LANES)
                tile = jnp.take_along_axis(up[i * SUB : (i + 1) * SUB, at], flip, axis=0, mode="promise_in_bounds")
                centre[EDGE - (i + 1) * SUB : EDGE - i * SUB, at] = tile

    lay(times(whole(rows_c), whole(cols_a, 0)), times(whole(rows_s), whole(cols_b, 0)))
    for g in range(GROUPS):
        columns(g, 1)

    for j in range(PIECES):
        @pl.when(me != REDUCERS[j])
        def _():
            piece_copy(j).wait_send()

    @pl.when(reduces)
    def _():
        for z in range(DEPTH):
            @pl.when(my_z != z)
            def _():
                line_copy(z).wait_send()

        for s in range(PLANE):
            @pl.when(me != s)
            def _():
                done_copy(s).wait_send()

    for dr, dc in AROUND:
        @pl.when(inside(dr, dc))
        def _():
            weight_copy(dr, dc).wait_send()
            slot_of = w_all.at[place(dr, dc)]
            pltpu.make_async_copy(slot_of, slot_of, recv_w.at[place(dr, dc)]).wait()

    for dr, dc in AROUND:
        turn(place(dr, dc), w_all[place(dr, dc), 0], w_all[place(dr, dc), 1])


def image_kernel(
    w_ref, wave_v, turn_v, rim_wave, rows_c, rows_s, cols_a, cols_b, plain_c, plain_s, centre, rim, out_hbm,
    edge_a, edge_b, edge_r, edge_i, image, out_sem,
):
    f32, i32, bf16 = jnp.float32, jnp.int32, jnp.bfloat16

    def store(n, source, rows, cols):
        copy = pltpu.make_async_copy(source, out_hbm.at[pl.ds(*rows), pl.ds(*cols)], out_sem.at[n])
        copy.start()
        return copy

    stores = [store(0, centre, (M, 2 * EDGE), (LANES, WIDE))]
    low = lax.broadcasted_iota(i32, (LOW, LANES), 0)
    lowf = low.astype(f32)

    def turned(g, h, real, imag):
        bc, bs = turn_v[0, g, h - 1 : h, :], turn_v[1, g, h - 1 : h, :]
        rc, ix, rs, ic = real * bc, imag * bs, real * bs, imag * bc
        return {h: (rc - ix, ic + rs), -h: (rc + ix, ic - rs)}

    def weighted(g, f, lc, ls):
        w_r, w_i = w_ref[2 * f, pl.ds(g, 1), :], w_ref[2 * f + 1, pl.ds(g, 1), :]
        return w_r * lc - w_i * ls, w_r * ls + w_i * lc

    def keep(g, block, own):
        at = slice(block * LOW, (block + 1) * LOW)
        edge_a[g, at, :] = own[0].astype(bf16)
        edge_b[g, at, :] = own[1].astype(bf16)

    def shared(g):
        lc, ls = wave_v[0, g], wave_v[1, g]
        z_r, z_i = weighted(g, 4, lc, ls)
        for f, side in ((3, (-8, -7)), (5, (6, 7))):
            s_r, s_i = weighted(g, f, lc, ls)
            d_r, d_i = z_r - s_r, z_i - s_i
            for b in side:
                start = (b + 8) * LOW
                if b < 0:
                    taper = (lowf + (start + M + 0.5)) * (1 / (2 * M))
                else:
                    taper = (C + M - 0.5 - start - lowf) * (1 / (2 * M))
                keep(g, MARGIN.index(b), turned(g, abs(b), s_r + taper * d_r, s_i + taper * d_i)[b])

    def edges(g, side):
        for half in range(M // LOW):
            at_half = slice(half * LOW, (half + 1) * LOW)
            c, s = rim_wave[0, g, at_half, :], rim_wave[1, g, at_half, :]
            for f, sign, at in ((side, -1.0, half * LOW), (6 + side, 1.0, M + half * LOW)):
                w_r, w_i = w_ref[2 * f, pl.ds(g, 1), :], w_ref[2 * f + 1, pl.ds(g, 1), :]
                if sign > 0:
                    real, imag = w_r * c - w_i * s, w_r * s + w_i * c
                else:
                    real, imag = w_r * c + w_i * s, w_i * c - w_r * s
                edge_r[side, g, at : at + LOW, :] = real.astype(bf16)
                edge_i[side, g, at : at + LOW, :] = imag.astype(bf16)

    def whole(ref, at=None):
        return jnp.concatenate([ref[g] if at is None else ref[at, g] for g in range(GROUPS)], 1)

    def times(rows, cols):
        return lax.dot_general(rows, cols, (((1,), (1,)), ((), ())), preferred_element_type=f32)

    d = lax.broadcasted_iota(i32, (M, 1), 0).astype(f32)
    t_own = (2 * M - 0.5 - d) * (1 / (2 * M))
    t_next = (d + 0.5) * (1 / (2 * M))
    flip = SUB - 1 - lax.broadcasted_iota(i32, (SUB, LANES), 0)

    def lay(down, up, start):
        to = slice(start, start + LANES)
        image[HALF : R - M, to] = down[:EDGE]
        for i in range(EDGE // SUB):
            tile = jnp.take_along_axis(up[i * SUB : (i + 1) * SUB], flip, axis=0, mode="promise_in_bounds")
            image[HALF - (i + 1) * SUB : HALF - i * SUB, to] = tile

    def seam(up, down, strip, start):
        to = slice(start, start + LANES)
        top = up * t_own + strip[:M] * t_next
        image[R - M :, to] = down * t_own + strip[M:] * t_next
        for i in range(M // SUB):
            tile = jnp.take_along_axis(top[i * SUB : (i + 1) * SUB], flip, axis=0, mode="promise_in_bounds")
            image[M - (i + 1) * SUB : M - i * SUB, to] = tile

    for g in range(GROUPS):
        shared(g)
        for side in range(3):
            edges(g, side)

    column = lax.broadcasted_iota(i32, (1, WIDE), 1)
    column = jnp.where(column < LANES, column, column + C - WIDE).astype(f32)
    t_mid = jnp.minimum(jnp.minimum((column + (M + 0.5)) * (1 / (2 * M)), (C + M - 0.5 - column) * (1 / (2 * M))), 1.0)
    t_left = jnp.maximum(M - 0.5 - column, 0.0) * (1 / (2 * M))
    t_right = jnp.maximum(column - (C - M - 0.5), 0.0) * (1 / (2 * M))

    def strips(sides, spot):
        real = jnp.concatenate([whole(edge_r, side) for side in sides], 0)
        imag = jnp.concatenate([whole(edge_i, side) for side in sides], 0)
        return times(real, whole(plain_c, spot)) - times(imag, whole(plain_s, spot))

    def outer_cols(inner_ref, edge_ref):
        parts = []
        for g in range(GROUPS):
            own = inner_ref[1, g]
            parts.append(jnp.concatenate([edge_ref[g, : 2 * LOW], own[2 * LOW : 6 * LOW], edge_ref[g, 2 * LOW :]], 0))
        return jnp.concatenate(parts, 1)

    even = times(whole(rows_c), outer_cols(cols_a, edge_a))
    odd = times(whole(rows_s), outer_cols(cols_b, edge_b))
    down, up = even - odd, even + odd
    for k, start in ((0, 0), (1, C - LANES)):
        at = slice(k * LANES, (k + 1) * LANES)
        lay(down[:EDGE, at], up[:EDGE, at], start)
        stores.append(store(1 + k, image.at[pl.ds(M, 2 * EDGE), pl.ds(start, LANES)], (M, 2 * EDGE), (start, LANES)))
    strip = strips((1,), 0)
    for k in range(2):
        at = slice(k * LANES, (k + 1) * LANES)
        seam(rim[0, :, at], rim[1, :, at], strip[:, at], (k + 1) * LANES)
    strip = strips((0, 1, 2), 1)
    strip = strip[: 2 * M] * t_left + strip[2 * M : 4 * M] * t_mid + strip[4 * M :] * t_right
    for k, start in ((0, 0), (1, C - LANES)):
        at = slice(k * LANES, (k + 1) * LANES)
        seam(up[EDGE:, at], down[EDGE:, at], strip[:, at], start)
    for n, row in ((3, 0), (4, R - M)):
        stores.append(store(n, image.at[pl.ds(row, M)], (row, M), (0, C)))
    for copy in stores:
        copy.wait()


def tile_of(order, vis, pairs, slot, ucell, vcell, gain):
    dma, vmem = pltpu.SemaphoreType.DMA, pltpu.VMEM
    f32, i32, bf16 = jnp.float32, jnp.int32, jnp.bfloat16
    inside = pl.BlockSpec(memory_space=pltpu.VMEM)
    kept = (
        vmem((18, SUB, LANES), f32),
        vmem((2, GROUPS, LOW, LANES), f32),
        vmem((2, GROUPS, SUB, LANES), f32),
        vmem((2, GROUPS, M, LANES), f32),
        vmem((GROUPS, HALF, LANES), bf16),
        vmem((GROUPS, HALF, LANES), bf16),
        vmem((2, GROUPS, WIDE, LANES), bf16),
        vmem((2, GROUPS, WIDE, LANES), bf16),
        vmem((2, GROUPS, WIDE, LANES), bf16),
        vmem((2, GROUPS, WIDE, LANES), bf16),
        vmem((2 * EDGE, WIDE), f32),
        vmem((2, M, WIDE), f32),
    )
    tables = pl.pallas_call(
        exchange_kernel,
        out_shape=kept,
        in_specs=[pl.BlockSpec(memory_space=pltpu.HBM)] * 7,
        out_specs=(inside,) * len(kept),
        scratch_shapes=[
            pltpu.SMEM((N_FROW * N_FCOL,), i32),
            vmem((2, BLOCK), f32),
            vmem((2, BLOCK), i32),
            vmem((1, BLOCK), i32),
            vmem((4, LANES), i32),
            vmem((4, LANES), i32),
            vmem((2 * GAIN_ROWS, LANES), f32),
            vmem((PIECES, 1, LANES), f32),
            vmem((PLANE, 1, LANES), f32),
            vmem((NBLK, LANES), f32),
            vmem((DEPTH, NBLK, LANES), f32),
            vmem((PIECES, NBLK, LANES), f32),
            vmem((2, SUB, LANES), f32),
            vmem((9, 2, SUB, LANES), f32),
            vmem((2, SUB, LANES), i32),
            vmem((2, SUB, LANES), f32),
            vmem((2, LOW // SUB - 1, 2, SUB, LANES), f32),
            dma((7,)), dma((PIECES,)), dma, dma((DEPTH,)), dma, dma((PLANE,)), dma, dma((9,)), dma((9,)),
        ],
        compiler_params=pltpu.CompilerParams(collective_id=0, has_side_effects=True, vmem_limit_bytes=24 * 1024 * 1024),
        name="exchange",
    )(*[pltpu.with_memory_space_constraint(x, pltpu.HBM) for x in (order, vis, pairs, slot, ucell, vcell, gain)])
    return pl.pallas_call(
        image_kernel,
        out_shape=jax.ShapeDtypeStruct((R, C), f32),
        in_specs=[inside] * len(kept),
        out_specs=pl.BlockSpec(memory_space=pl.ANY),
        scratch_shapes=[
            vmem((GROUPS, 2 * M, LANES), bf16),
            vmem((GROUPS, 2 * M, LANES), bf16),
            vmem((3, GROUPS, 2 * M, LANES), bf16),
            vmem((3, GROUPS, 2 * M, LANES), bf16),
            vmem((R, C), f32),
            dma((5,)),
        ],
        compiler_params=pltpu.CompilerParams(vmem_limit_bytes=24 * 1024 * 1024),
        name="image",
    )(*tables)


def shards(vis, station_pairs, visibility_time_slot, station_u_cells, station_v_cells, facet_station_gains, holder_device_order):
    gains = facet_station_gains.reshape(2, GAIN_ROWS, LANES).transpose(1, 0, 2).reshape(2 * GAIN_ROWS, LANES)
    return tile_of(
        holder_device_order, vis, station_pairs, visibility_time_slot.reshape(1, BLOCK),
        station_u_cells.reshape(4, LANES), station_v_cells.reshape(4, LANES), gains,
    )


def solution(mesh):
    return jax.shard_map(
        shards,
        mesh=mesh,
        in_specs=(
            P(None, ("frow", "fcol")),
            P(None, ("frow", "fcol")),
            P(("frow", "fcol")),
            P(),
            P(),
            P("frow", "fcol", None, None),
            P(),
        ),
        out_specs=P("frow", "fcol"),
        check_vma=False,
    )
```

```python
import math

import jax
import jax.numpy as jnp
from jax import lax
from jax.experimental import pallas as pl
from jax.experimental.pallas import tpu as pltpu
from jax.sharding import PartitionSpec as P

R = 1024
C = 512
M = 64
NT = 16
NBLK = 4
BLOCK = 256
K = NBLK * BLOCK
N_FROW = 16
N_FCOL = 32
LANES = 128
SUB = 8
GROUPS = K // LANES
SIZE = R * N_FROW
PLANE = 32
DEPTH = 16
PIECES = 10
REDUCERS = tuple(6 * (j // 2) + j % 2 for j in range(PIECES))
PEERS = REDUCERS + tuple(s for s in range(PLANE) if s not in REDUCERS)
GAIN_ROWS = 64
MESH = pl.DeviceIdType.MESH
NEAR = [(-1, 0), (1, 0)]
FAR = [(dr, dc) for dc in (-1, 1) for dr in (-1, 1, 0)]
AROUND = FAR + NEAR


def place(dr, dc):
    return (1 + dr) * 3 + 1 + dc


def circle(m):
    m = m & (2 * SIZE - 1)
    quarter = (m + SIZE // 4) >> 13
    x = (m - (quarter << 13)).astype(jnp.float32) * (math.pi / SIZE)
    x2 = x * x
    s = x * (1.0 + x2 * (-1 / 6 + x2 * (1 / 120 + x2 * (-1 / 5040 + x2 * (1 / 362880)))))
    c = 1.0 + x2 * (-1 / 2 + x2 * (1 / 24 + x2 * (-1 / 720 + x2 * (1 / 40320))))
    odd = (quarter & 1) == 1
    cos = jnp.where(odd, s, c)
    sin = jnp.where(odd, c, s)
    cos = jnp.where(((quarter + 1) & 2) == 2, -cos, cos)
    sin = jnp.where((quarter & 2) == 2, -sin, sin)
    return cos, sin


def take_lanes(row, index):
    return jnp.take_along_axis(row, index, axis=1, mode="promise_in_bounds")


HALF = R // 2
LOW = 32
WIDE = 256
EDGE = HALF - M
INNER = tuple(range(-4, 4))
MARGIN = (-8, -7, 6, 7)
OUTER = tuple(range(-8, -4)) + tuple(range(4, 8))


def exchange_kernel(
    order_hbm, vis_hbm, pairs_hbm, slot_hbm, ucell_hbm, vcell_hbm, gain_hbm,
    w_ref, wave_v, turn_v, rim_wave, rows_c, rows_s, cols_a, cols_b, plain_c, plain_s, centre, edge_r, edge_i,
    order, vis, pairs, slot, ucell, vcell, gain, pay, raw, part, line, done, w_own, w_all, uv_ref, turn_u, spin, rim,
    in_sem, send1, recv1, send2, recv2, send3, recv3, send_w, recv_w,
):
    fr, fc = lax.axis_index("frow"), lax.axis_index("fcol")
    f32, i32, bf16 = jnp.float32, jnp.int32, jnp.bfloat16
    z_lo, y = lax.div(fr, 4), lax.rem(fr, 4)
    z_hi, xc = lax.div(fc, 8), lax.rem(fc, 8)
    me = y * 8 + xc
    my_z = z_hi * 4 + z_lo
    mine = 2 * lax.div(me, 6) + lax.rem(me, 6)
    reduces = jnp.logical_and(lax.rem(me, 6) < 2, mine < PIECES)
    plane_row, plane_col = z_lo * 4, z_hi * 8

    def in_plane(s):
        return (plane_row + s // 8, plane_col + s % 8)

    def in_line(z):
        return ((z % 4) * 4 + y, (z // 4) * 8 + xc)

    def inside(dr, dc):
        row, col = fr + dr, fc + dc
        return (row >= 0) & (row < N_FROW) & (col >= 0) & (col < N_FCOL)

    loads = ((vis_hbm, vis), (pairs_hbm, pairs), (slot_hbm, slot), (order_hbm, order), (ucell_hbm, ucell), (vcell_hbm, vcell), (gain_hbm, gain))
    loads = [pltpu.make_async_copy(a, b, in_sem.at[n]) for n, (a, b) in enumerate(loads)]
    for load in loads[:4]:
        load.start()
    barrier = pltpu.get_barrier_semaphore()

    def greet(device):
        pl.semaphore_signal(barrier, inc=1, device_id=device, device_id_type=MESH)

    @pl.when(reduces)
    def _():
        for z in range(DEPTH):
            @pl.when(my_z != z)
            def _():
                greet(in_line(z))

        for s in range(PLANE):
            @pl.when(me != s)
            def _():
                greet(in_plane(s))

    @pl.when(jnp.logical_not(reduces))
    def _():
        for j in range(PIECES):
            greet(in_plane(REDUCERS[j]))

    count = jnp.where(reduces, PLANE - 1 + DEPTH - 1, PIECES)
    for dr, dc in AROUND:
        count = count + inside(dr, dc).astype(i32)

        @pl.when(inside(dr, dc))
        def _():
            greet((fr + dr, fc + dc))

    for load in loads[4:]:
        load.start()
    for dr, dc in AROUND:
        @pl.when(jnp.logical_not(inside(dr, dc)))
        def _():
            w_all[place(dr, dc)] = jnp.zeros((2, SUB, LANES), f32)

    for load in loads[:4]:
        load.wait()
    for half in range(2):
        cols = slice(half * LANES, (half + 1) * LANES)
        pay[half] = vis[0:1, cols]
        pay[2 + half] = vis[1:2, cols]
        pay[4 + half] = pairs[0:1, cols].astype(f32)
        pay[6 + half] = pairs[1:2, cols].astype(f32)
        pay[8 + half] = slot[0:1, cols].astype(f32)

    pl.semaphore_wait(barrier, count)

    def piece_copy(j):
        return pltpu.make_async_remote_copy(
            src_ref=pay.at[j], dst_ref=raw.at[me], send_sem=send1.at[j], recv_sem=recv1,
            device_id=in_plane(REDUCERS[j]), device_id_type=MESH,
        )

    def line_copy(z):
        return pltpu.make_async_remote_copy(
            src_ref=part, dst_ref=line.at[my_z], send_sem=send2.at[z], recv_sem=recv2,
            device_id=in_line(z), device_id_type=MESH,
        )

    def done_copy(s):
        return pltpu.make_async_remote_copy(
            src_ref=done.at[mine], dst_ref=done.at[mine], send_sem=send3.at[s], recv_sem=recv3,
            device_id=in_plane(s), device_id_type=MESH,
        )

    def weight_copy(dr, dc):
        return pltpu.make_async_remote_copy(
            src_ref=w_own, dst_ref=w_all.at[place(-dr, -dc)],
            send_sem=send_w.at[place(dr, dc)], recv_sem=recv_w.at[place(-dr, -dc)],
            device_id=(fr + dr, fc + dc), device_id_type=MESH,
        )

    def landed(ref, slots, sem):
        view = ref.at[pl.ds(0, slots)]
        pltpu.make_async_copy(view, view, sem).wait()

    for j in range(PIECES):
        @pl.when(me != REDUCERS[j])
        def _():
            piece_copy(j).start()

    @pl.when(reduces)
    def _():
        raw[me] = pay[mine]
        s = lax.broadcasted_iota(i32, (PLANE, 1, LANES), 0)
        holder = (plane_row + (s >> 3)) * N_FCOL + plane_col + (s & 7)
        landed(raw, PLANE - 1, recv1)
        values = raw[...]
        for b in range(NBLK):
            part[b : b + 1, :] = jnp.sum(jnp.where(holder == order[b], values, 0.0), axis=0)
        for z in range(DEPTH):
            @pl.when(my_z != z)
            def _():
                line_copy(z).start()

        line[my_z] = part[...]
        landed(line, DEPTH - 1, recv2)
        done[mine] = jnp.sum(line[...], axis=0)
        for s in PEERS:
            @pl.when(me != s)
            def _():
                done_copy(s).start()

        landed(done, PIECES - 1, recv3)

    @pl.when(jnp.logical_not(reduces))
    def _():
        landed(done, PIECES, recv3)

    for load in loads[4:]:
        load.wait()

    def value(v):
        return jnp.concatenate([done[2 * v], done[2 * v + 1]], 0)

    s1, s2, t = value(2).astype(i32), value(3).astype(i32), value(4).astype(i32)
    first, second = s1 * NT + t, s2 * NT + t

    def pick(part, index):
        lane, row = index & 127, index >> 7
        bits = [(row & (1 << b)) != 0 for b in range(6)]
        stack = []
        for n in range(GAIN_ROWS):
            values = jnp.broadcast_to(gain[2 * n + part : 2 * n + part + 1, :], (SUB, LANES))
            found, level = take_lanes(values, lane), 0
            while stack and stack[-1][0] == level:
                found = jnp.where(bits[level], found, stack.pop()[1])
                level += 1
            stack.append((level, found))
        return stack[0][1]

    scale = 0.5 / math.sqrt(K)
    v_r, v_i = value(0), value(1)
    g1r, g1i = pick(0, first), pick(1, first)
    g2r, g2i = pick(0, second), pick(1, second)
    real_gain = g1r * g2r + g1i * g2i
    imag_gain = g1i * g2r - g1r * g2i
    w_own[0] = scale * (v_r * real_gain - v_i * imag_gain)
    w_own[1] = scale * (v_r * imag_gain + v_i * real_gain)
    for dr, dc in AROUND:
        @pl.when(inside(dr, dc))
        def _():
            weight_copy(dr, dc).start()

    def station(ref):
        total = jnp.zeros((SUB, LANES), i32)
        for row in range(4):
            cells = jnp.broadcast_to(ref[row : row + 1, :], (SUB, LANES))
            one = take_lanes(cells, s1 & 127)
            two = take_lanes(cells, s2 & 127)
            total = total + jnp.where((s1 >> 7) == row, one, 0) - jnp.where((s2 >> 7) == row, two, 0)
        return total

    u, v = station(ucell), station(vcell)
    uv_ref[0] = u
    uv_ref[1] = v
    mid_c, mid_s = circle(u * (fr * (2 * R) + R - 1) + v * (2 * (fc * C + C // 2)))

    def turn(place_of, w_r, w_i):
        w_ref[2 * place_of] = w_r * mid_c - w_i * mid_s
        w_ref[2 * place_of + 1] = w_r * mid_s + w_i * mid_c

    turn(4, w_own[0], w_own[1])

    low = lax.broadcasted_iota(i32, (LOW, LANES), 0)
    step = lax.broadcasted_iota(i32, (SUB, LANES), 0) + 1

    for n, cells in enumerate((uv_ref[0], uv_ref[1])):
        for i in range(1, LOW // SUB):
            spin[n, i - 1, 0], spin[n, i - 1, 1] = circle(cells * (2 * SUB * i))

    def fan(n, g, c, s):
        cos, sin = [c], [s]
        for i in range(LOW // SUB - 1):
            bc, bs = spin[n, i, 0, pl.ds(g, 1), :], spin[n, i, 1, pl.ds(g, 1), :]
            cos.append(c * bc - s * bs)
            sin.append(s * bc + c * bs)
        return jnp.concatenate(cos, 0), jnp.concatenate(sin, 0)

    def row_tables(g):
        u = uv_ref[0, pl.ds(g, 1), :]
        v = uv_ref[1, pl.ds(g, 1), :]
        lc, ls = fan(0, g, *circle(u * (2 * step - 1 + HALF)))
        hc, hs = circle(u * (2 * LOW * step))
        turn_u[0] = hc
        turn_u[1] = hs

        def put(block, c, s):
            at = slice((block + 8) * LOW, (block + 9) * LOW)
            rows_c[g, at, :] = c.astype(bf16)
            rows_s[g, at, :] = s.astype(bf16)
            if block >= 6:
                rim_wave[0, g, (block - 6) * LOW : (block - 5) * LOW, :] = c
                rim_wave[1, g, (block - 6) * LOW : (block - 5) * LOW, :] = s

        put(0, lc, ls)
        for h in range(1, 9):
            bc, bs = turn_u[0, h - 1 : h, :], turn_u[1, h - 1 : h, :]
            cc, ss, cs, sc = lc * bc, ls * bs, lc * bs, ls * bc
            put(-h, cc + ss, sc - cs)
            if h < 8:
                put(h, cc - ss, sc + cs)
        lc, ls = fan(1, g, *circle(v * (2 * step - 2)))
        wave_v[0, g] = lc
        wave_v[1, g] = ls
        hc, hs = circle(v * (2 * LOW * step))
        turn_v[0, g] = hc
        turn_v[1, g] = hs

    def prepare(n, carry):
        row_tables(n)
        return carry

    lax.fori_loop(0, GROUPS, prepare, 0)

    lowf = low.astype(f32)

    def turned(g, h, real, imag):
        bc, bs = turn_v[0, g, h - 1 : h, :], turn_v[1, g, h - 1 : h, :]
        rc, ix, rs, ic = real * bc, imag * bs, real * bs, imag * bc
        return {h: (rc - ix, ic + rs), -h: (rc + ix, ic - rs)}

    def weighted(g, f, lc, ls):
        w_r, w_i = w_ref[2 * f, pl.ds(g, 1), :], w_ref[2 * f + 1, pl.ds(g, 1), :]
        return w_r * lc - w_i * ls, w_r * ls + w_i * lc

    def keep(g, spot, block, own, plain):
        at = slice(block * LOW, (block + 1) * LOW)
        if own is not None:
            cols_a[spot, g, at, :] = own[0].astype(bf16)
            cols_b[spot, g, at, :] = own[1].astype(bf16)
        if plain is not None:
            plain_c[spot, g, at, :] = plain[0].astype(bf16)
            plain_s[spot, g, at, :] = plain[1].astype(bf16)

    def columns(g, spot):
        blocks = (INNER, OUTER)[spot]
        lc, ls = wave_v[0, g], wave_v[1, g]
        z_r, z_i = weighted(g, 4, lc, ls)
        plain = {0: (lc, ls)}
        own = {0: (z_r, z_i)}
        for h in sorted({abs(b) for b in blocks} - {0}):
            plain.update(turned(g, h, lc, ls))
            if h < 7:
                own.update(turned(g, h, z_r, z_i))
        for n, b in enumerate(blocks):
            keep(g, spot, n, own[b] if -7 < b < 6 else None, plain[b])

    def inner(g, carry):
        columns(g, 0)
        return carry

    lax.fori_loop(0, GROUPS, inner, 0)

    def whole(ref, at=None):
        return jnp.concatenate([ref[g] if at is None else ref[at, g] for g in range(GROUPS)], 1)

    def times(rows, cols):
        return lax.dot_general(rows, cols, (((1,), (1,)), ((), ())), preferred_element_type=f32)

    flip = SUB - 1 - lax.broadcasted_iota(i32, (SUB, LANES), 0)

    d = lax.broadcasted_iota(i32, (M, 1), 0).astype(f32)
    t_own = (2 * M - 0.5 - d) * (1 / (2 * M))
    t_next = (d + 0.5) * (1 / (2 * M))
    def edges(g, side):
        for half in range(M // LOW):
            at_half = slice(half * LOW, (half + 1) * LOW)
            c, s = rim_wave[0, g, at_half, :], rim_wave[1, g, at_half, :]
            for f, sign, at in ((side, -1.0, half * LOW), (6 + side, 1.0, M + half * LOW)):
                w_r, w_i = w_ref[2 * f, pl.ds(g, 1), :], w_ref[2 * f + 1, pl.ds(g, 1), :]
                if sign > 0:
                    real, imag = w_r * c - w_i * s, w_r * s + w_i * c
                else:
                    real, imag = w_r * c + w_i * s, w_i * c - w_r * s
                edge_r[g, at : at + LOW, :] = real.astype(bf16)
                edge_i[g, at : at + LOW, :] = imag.astype(bf16)

    def lay(even, odd):
        down = even - odd
        up = even + odd
        rim[0] = up[EDGE:]
        rim[1] = down[EDGE:]
        centre[HALF : R - M, :] = down[:EDGE]
        for i in range(EDGE // SUB):
            for k in range(WIDE // LANES):
                at = slice(k * LANES, (k + 1) * LANES)
                tile = jnp.take_along_axis(up[i * SUB : (i + 1) * SUB, at], flip, axis=0, mode="promise_in_bounds")
                centre[HALF - (i + 1) * SUB : HALF - i * SUB, at] = tile

    lay(times(whole(rows_c), whole(cols_a, 0)), times(whole(rows_s), whole(cols_b, 0)))
    for g in range(GROUPS):
        columns(g, 1)

    def come(dr, dc):
        @pl.when(inside(dr, dc))
        def _():
            slot_of = w_all.at[place(dr, dc)]
            pltpu.make_async_copy(slot_of, slot_of, recv_w.at[place(dr, dc)]).wait()

    for dr, dc in NEAR:
        come(dr, dc)
    for dr, dc in NEAR:
        turn(place(dr, dc), w_all[place(dr, dc), 0], w_all[place(dr, dc), 1])
    for g in range(GROUPS):
        edges(g, 1)
    strip = times(whole(edge_r), whole(plain_c, 0)) - times(whole(edge_i), whole(plain_s, 0))
    top = rim[0] * t_own + strip[:M] * t_next
    centre[R - M :, :] = rim[1] * t_own + strip[M:] * t_next
    for i in range(M // SUB):
        for k in range(WIDE // LANES):
            at = slice(k * LANES, (k + 1) * LANES)
            tile = jnp.take_along_axis(top[i * SUB : (i + 1) * SUB, at], flip, axis=0, mode="promise_in_bounds")
            centre[M - (i + 1) * SUB : M - i * SUB, at] = tile

    for j in range(PIECES):
        @pl.when(me != REDUCERS[j])
        def _():
            piece_copy(j).wait_send()

    @pl.when(reduces)
    def _():
        for z in range(DEPTH):
            @pl.when(my_z != z)
            def _():
                line_copy(z).wait_send()

        for s in range(PLANE):
            @pl.when(me != s)
            def _():
                done_copy(s).wait_send()

    for dr, dc in AROUND:
        @pl.when(inside(dr, dc))
        def _():
            weight_copy(dr, dc).wait_send()

    for dr, dc in FAR:
        come(dr, dc)
    for dr, dc in FAR:
        turn(place(dr, dc), w_all[place(dr, dc), 0], w_all[place(dr, dc), 1])


def image_kernel(
    w_ref, wave_v, turn_v, rim_wave, rows_c, rows_s, cols_a, cols_b, plain_c, plain_s, centre, mid_r, mid_i, out_hbm,
    edge_a, edge_b, edge_r, edge_i, image, out_sem,
):
    f32, i32, bf16 = jnp.float32, jnp.int32, jnp.bfloat16

    def store(n, source, rows, cols):
        copy = pltpu.make_async_copy(source, out_hbm.at[pl.ds(*rows), pl.ds(*cols)], out_sem.at[n])
        copy.start()
        return copy

    stores = [store(0, centre, (0, R), (LANES, WIDE))]
    low = lax.broadcasted_iota(i32, (LOW, LANES), 0)
    lowf = low.astype(f32)

    def turned(g, h, real, imag):
        bc, bs = turn_v[0, g, h - 1 : h, :], turn_v[1, g, h - 1 : h, :]
        rc, ix, rs, ic = real * bc, imag * bs, real * bs, imag * bc
        return {h: (rc - ix, ic + rs), -h: (rc + ix, ic - rs)}

    def weighted(g, f, lc, ls):
        w_r, w_i = w_ref[2 * f, pl.ds(g, 1), :], w_ref[2 * f + 1, pl.ds(g, 1), :]
        return w_r * lc - w_i * ls, w_r * ls + w_i * lc

    def keep(g, block, own):
        at = slice(block * LOW, (block + 1) * LOW)
        edge_a[g, at, :] = own[0].astype(bf16)
        edge_b[g, at, :] = own[1].astype(bf16)

    def shared(g):
        lc, ls = wave_v[0, g], wave_v[1, g]
        z_r, z_i = weighted(g, 4, lc, ls)
        for f, side in ((3, (-8, -7)), (5, (6, 7))):
            s_r, s_i = weighted(g, f, lc, ls)
            d_r, d_i = z_r - s_r, z_i - s_i
            for b in side:
                start = (b + 8) * LOW
                if b < 0:
                    taper = (lowf + (start + M + 0.5)) * (1 / (2 * M))
                else:
                    taper = (C + M - 0.5 - start - lowf) * (1 / (2 * M))
                keep(g, MARGIN.index(b), turned(g, abs(b), s_r + taper * d_r, s_i + taper * d_i)[b])

    def edges(g, side):
        for half in range(M // LOW):
            at_half = slice(half * LOW, (half + 1) * LOW)
            c, s = rim_wave[0, g, at_half, :], rim_wave[1, g, at_half, :]
            for f, sign, at in ((side, -1.0, half * LOW), (6 + side, 1.0, M + half * LOW)):
                w_r, w_i = w_ref[2 * f, pl.ds(g, 1), :], w_ref[2 * f + 1, pl.ds(g, 1), :]
                if sign > 0:
                    real, imag = w_r * c - w_i * s, w_r * s + w_i * c
                else:
                    real, imag = w_r * c + w_i * s, w_i * c - w_r * s
                edge_r[side // 2, g, at : at + LOW, :] = real.astype(bf16)
                edge_i[side // 2, g, at : at + LOW, :] = imag.astype(bf16)

    def whole(ref, at=None):
        return jnp.concatenate([ref[g] if at is None else ref[at, g] for g in range(GROUPS)], 1)

    def times(rows, cols):
        return lax.dot_general(rows, cols, (((1,), (1,)), ((), ())), preferred_element_type=f32)

    d = lax.broadcasted_iota(i32, (M, 1), 0).astype(f32)
    t_own = (2 * M - 0.5 - d) * (1 / (2 * M))
    t_next = (d + 0.5) * (1 / (2 * M))
    flip = SUB - 1 - lax.broadcasted_iota(i32, (SUB, LANES), 0)

    def lay(down, up, start):
        to = slice(start, start + LANES)
        image[HALF : R - M, to] = down[:EDGE]
        for i in range(EDGE // SUB):
            tile = jnp.take_along_axis(up[i * SUB : (i + 1) * SUB], flip, axis=0, mode="promise_in_bounds")
            image[HALF - (i + 1) * SUB : HALF - i * SUB, to] = tile

    def seam(up, down, strip, start):
        to = slice(start, start + LANES)
        top = up * t_own + strip[:M] * t_next
        image[R - M :, to] = down * t_own + strip[M:] * t_next
        for i in range(M // SUB):
            tile = jnp.take_along_axis(top[i * SUB : (i + 1) * SUB], flip, axis=0, mode="promise_in_bounds")
            image[M - (i + 1) * SUB : M - i * SUB, to] = tile

    for g in range(GROUPS):
        shared(g)
        for side in (0, 2):
            edges(g, side)

    column = lax.broadcasted_iota(i32, (1, WIDE), 1)
    column = jnp.where(column < LANES, column, column + C - WIDE).astype(f32)
    t_mid = jnp.minimum(jnp.minimum((column + (M + 0.5)) * (1 / (2 * M)), (C + M - 0.5 - column) * (1 / (2 * M))), 1.0)
    t_left = jnp.maximum(M - 0.5 - column, 0.0) * (1 / (2 * M))
    t_right = jnp.maximum(column - (C - M - 0.5), 0.0) * (1 / (2 * M))

    def strips():
        real = jnp.concatenate([whole(edge_r, 0), whole(mid_r), whole(edge_r, 1)], 0)
        imag = jnp.concatenate([whole(edge_i, 0), whole(mid_i), whole(edge_i, 1)], 0)
        return times(real, whole(plain_c, 1)) - times(imag, whole(plain_s, 1))

    def outer_cols(inner_ref, edge_ref):
        parts = []
        for g in range(GROUPS):
            own = inner_ref[1, g]
            parts.append(jnp.concatenate([edge_ref[g, : 2 * LOW], own[2 * LOW : 6 * LOW], edge_ref[g, 2 * LOW :]], 0))
        return jnp.concatenate(parts, 1)

    even = times(whole(rows_c), outer_cols(cols_a, edge_a))
    odd = times(whole(rows_s), outer_cols(cols_b, edge_b))
    down, up = even - odd, even + odd
    for k, start in ((0, 0), (1, C - LANES)):
        at = slice(k * LANES, (k + 1) * LANES)
        lay(down[:EDGE, at], up[:EDGE, at], start)
        stores.append(store(1 + k, image.at[pl.ds(M, 2 * EDGE), pl.ds(start, LANES)], (M, 2 * EDGE), (start, LANES)))
    strip = strips()
    strip = strip[: 2 * M] * t_left + strip[2 * M : 4 * M] * t_mid + strip[4 * M :] * t_right
    for k, start in ((0, 0), (1, C - LANES)):
        at = slice(k * LANES, (k + 1) * LANES)
        seam(up[EDGE:, at], down[EDGE:, at], strip[:, at], start)
    for n, row in ((3, 0), (5, R - M)):
        for k, start in ((0, 0), (1, C - LANES)):
            stores.append(store(n + k, image.at[pl.ds(row, M), pl.ds(start, LANES)], (row, M), (start, LANES)))
    for copy in stores:
        copy.wait()


def tile_of(order, vis, pairs, slot, ucell, vcell, gain):
    dma, vmem = pltpu.SemaphoreType.DMA, pltpu.VMEM
    f32, i32, bf16 = jnp.float32, jnp.int32, jnp.bfloat16
    inside = pl.BlockSpec(memory_space=pltpu.VMEM)
    kept = (
        vmem((18, SUB, LANES), f32),
        vmem((2, GROUPS, LOW, LANES), f32),
        vmem((2, GROUPS, SUB, LANES), f32),
        vmem((2, GROUPS, M, LANES), f32),
        vmem((GROUPS, HALF, LANES), bf16),
        vmem((GROUPS, HALF, LANES), bf16),
        vmem((2, GROUPS, WIDE, LANES), bf16),
        vmem((2, GROUPS, WIDE, LANES), bf16),
        vmem((2, GROUPS, WIDE, LANES), bf16),
        vmem((2, GROUPS, WIDE, LANES), bf16),
        vmem((R, WIDE), f32),
        vmem((GROUPS, 2 * M, LANES), bf16),
        vmem((GROUPS, 2 * M, LANES), bf16),
    )
    tables = pl.pallas_call(
        exchange_kernel,
        out_shape=kept,
        in_specs=[pl.BlockSpec(memory_space=pltpu.HBM)] * 7,
        out_specs=(inside,) * len(kept),
        scratch_shapes=[
            pltpu.SMEM((N_FROW * N_FCOL,), i32),
            vmem((2, BLOCK), f32),
            vmem((2, BLOCK), i32),
            vmem((1, BLOCK), i32),
            vmem((4, LANES), i32),
            vmem((4, LANES), i32),
            vmem((2 * GAIN_ROWS, LANES), f32),
            vmem((PIECES, 1, LANES), f32),
            vmem((PLANE, 1, LANES), f32),
            vmem((NBLK, LANES), f32),
            vmem((DEPTH, NBLK, LANES), f32),
            vmem((PIECES, NBLK, LANES), f32),
            vmem((2, SUB, LANES), f32),
            vmem((9, 2, SUB, LANES), f32),
            vmem((2, SUB, LANES), i32),
            vmem((2, SUB, LANES), f32),
            vmem((2, LOW // SUB - 1, 2, SUB, LANES), f32),
            vmem((2, M, WIDE), f32),
            dma((7,)), dma((PIECES,)), dma, dma((DEPTH,)), dma, dma((PLANE,)), dma, dma((9,)), dma((9,)),
        ],
        compiler_params=pltpu.CompilerParams(collective_id=0, has_side_effects=True, vmem_limit_bytes=24 * 1024 * 1024),
        name="exchange",
    )(*[pltpu.with_memory_space_constraint(x, pltpu.HBM) for x in (order, vis, pairs, slot, ucell, vcell, gain)])
    return pl.pallas_call(
        image_kernel,
        out_shape=jax.ShapeDtypeStruct((R, C), f32),
        in_specs=[inside] * len(kept),
        out_specs=pl.BlockSpec(memory_space=pl.ANY),
        scratch_shapes=[
            vmem((GROUPS, 2 * M, LANES), bf16),
            vmem((GROUPS, 2 * M, LANES), bf16),
            vmem((2, GROUPS, 2 * M, LANES), bf16),
            vmem((2, GROUPS, 2 * M, LANES), bf16),
            vmem((R, C), f32),
            dma((7,)),
        ],
        compiler_params=pltpu.CompilerParams(vmem_limit_bytes=24 * 1024 * 1024),
        name="image",
    )(*tables)


def shards(vis, station_pairs, visibility_time_slot, station_u_cells, station_v_cells, facet_station_gains, holder_device_order):
    gains = facet_station_gains.reshape(2, GAIN_ROWS, LANES).transpose(1, 0, 2).reshape(2 * GAIN_ROWS, LANES)
    return tile_of(
        holder_device_order, vis, station_pairs, visibility_time_slot.reshape(1, BLOCK),
        station_u_cells.reshape(4, LANES), station_v_cells.reshape(4, LANES), gains,
    )


def solution(mesh):
    return jax.shard_map(
        shards,
        mesh=mesh,
        in_specs=(
            P(None, ("frow", "fcol")),
            P(None, ("frow", "fcol")),
            P(("frow", "fcol")),
            P(),
            P(),
            P("frow", "fcol", None, None),
            P(),
        ),
        out_specs=P("frow", "fcol"),
        check_vma=False,
    )
```

```python
import math

import jax
import jax.numpy as jnp
from jax import lax
from jax.experimental import pallas as pl
from jax.experimental.pallas import tpu as pltpu
from jax.sharding import PartitionSpec as P

R = 1024
C = 512
M = 64
NT = 16
NBLK = 4
BLOCK = 256
K = NBLK * BLOCK
N_FROW = 16
N_FCOL = 32
LANES = 128
SUB = 8
GROUPS = K // LANES
SIZE = R * N_FROW
PLANE = 32
DEPTH = 16
PIECES = 10
REDUCERS = tuple(6 * (j // 2) + j % 2 for j in range(PIECES))
PEERS = REDUCERS + tuple(s for s in range(PLANE) if s not in REDUCERS)
GAIN_ROWS = 64
MESH = pl.DeviceIdType.MESH
NEAR = [(-1, 0), (1, 0)]
FAR = [(dr, dc) for dc in (-1, 1) for dr in (-1, 1, 0)]
AROUND = FAR + NEAR


def place(dr, dc):
    return (1 + dr) * 3 + 1 + dc


def circle(m):
    m = m & (2 * SIZE - 1)
    quarter = (m + SIZE // 4) >> 13
    x = (m - (quarter << 13)).astype(jnp.float32) * (math.pi / SIZE)
    x2 = x * x
    s = x * (1.0 + x2 * (-1 / 6 + x2 * (1 / 120 + x2 * (-1 / 5040 + x2 * (1 / 362880)))))
    c = 1.0 + x2 * (-1 / 2 + x2 * (1 / 24 + x2 * (-1 / 720 + x2 * (1 / 40320))))
    odd = (quarter & 1) == 1
    cos = jnp.where(odd, s, c)
    sin = jnp.where(odd, c, s)
    cos = jnp.where(((quarter + 1) & 2) == 2, -cos, cos)
    sin = jnp.where((quarter & 2) == 2, -sin, sin)
    return cos, sin


def take_lanes(row, index):
    return jnp.take_along_axis(row, index, axis=1, mode="promise_in_bounds")


HALF = R // 2
LOW = 32
WIDE = 256
EDGE = HALF - M
INNER = tuple(range(-4, 4))
MARGIN = (-8, -7, 6, 7)
OUTER = tuple(range(-8, -4)) + tuple(range(4, 8))


def exchange_kernel(
    order_hbm, vis_hbm, pairs_hbm, slot_hbm, ucell_hbm, vcell_hbm, gain_hbm,
    w_ref, wave_v, turn_v, rim_wave, rows_c, rows_s, cols_a, cols_b, plain_c, plain_s, centre, edge_r, edge_i,
    order, vis, pairs, slot, ucell, vcell, gain, pay, raw, part, line, done, w_own, w_all, uv_ref, turn_u, spin, rim, sent,
    in_sem, send1, recv1, send2, recv2, send3, recv3, send_w, recv_w,
):
    fr, fc = lax.axis_index("frow"), lax.axis_index("fcol")
    f32, i32, bf16 = jnp.float32, jnp.int32, jnp.bfloat16
    z_lo, y = lax.div(fr, 4), lax.rem(fr, 4)
    z_hi, xc = lax.div(fc, 8), lax.rem(fc, 8)
    me = y * 8 + xc
    my_z = z_hi * 4 + z_lo
    mine = 2 * lax.div(me, 6) + lax.rem(me, 6)
    reduces = jnp.logical_and(lax.rem(me, 6) < 2, mine < PIECES)
    plane_row, plane_col = z_lo * 4, z_hi * 8

    def in_plane(s):
        return (plane_row + s // 8, plane_col + s % 8)

    def in_line(z):
        return ((z % 4) * 4 + y, (z // 4) * 8 + xc)

    def inside(dr, dc):
        row, col = fr + dr, fc + dc
        return (row >= 0) & (row < N_FROW) & (col >= 0) & (col < N_FCOL)

    loads = ((vis_hbm, vis), (pairs_hbm, pairs), (slot_hbm, slot), (order_hbm, order), (ucell_hbm, ucell), (vcell_hbm, vcell), (gain_hbm, gain))
    loads = [pltpu.make_async_copy(a, b, in_sem.at[n]) for n, (a, b) in enumerate(loads)]
    for load in loads[:4]:
        load.start()
    barrier = pltpu.get_barrier_semaphore()

    def greet(device):
        pl.semaphore_signal(barrier, inc=1, device_id=device, device_id_type=MESH)

    @pl.when(reduces)
    def _():
        for z in range(DEPTH):
            @pl.when(my_z != z)
            def _():
                greet(in_line(z))

        for s in range(PLANE):
            @pl.when(me != s)
            def _():
                greet(in_plane(s))

    @pl.when(jnp.logical_not(reduces))
    def _():
        for j in range(PIECES):
            greet(in_plane(REDUCERS[j]))

    count = jnp.where(reduces, PLANE - 1 + DEPTH - 1, PIECES)
    for dr, dc in AROUND:
        count = count + inside(dr, dc).astype(i32)

        @pl.when(inside(dr, dc))
        def _():
            greet((fr + dr, fc + dc))

    for load in loads[4:]:
        load.start()
    for dr, dc in AROUND:
        @pl.when(jnp.logical_not(inside(dr, dc)))
        def _():
            w_all[place(dr, dc)] = jnp.zeros((2, SUB, LANES), f32)

    for load in loads[:4]:
        load.wait()
    for half in range(2):
        cols = slice(half * LANES, (half + 1) * LANES)
        pay[half] = vis[0:1, cols]
        pay[2 + half] = vis[1:2, cols]
        pay[4 + half] = pairs[0:1, cols].astype(f32)
        pay[6 + half] = pairs[1:2, cols].astype(f32)
        pay[8 + half] = slot[0:1, cols].astype(f32)

    pl.semaphore_wait(barrier, count)

    def piece_copy(j):
        return pltpu.make_async_remote_copy(
            src_ref=pay.at[j], dst_ref=raw.at[me], send_sem=send1, recv_sem=recv1,
            device_id=in_plane(REDUCERS[j]), device_id_type=MESH,
        )

    def line_copy(z):
        return pltpu.make_async_remote_copy(
            src_ref=part, dst_ref=line.at[my_z], send_sem=send2, recv_sem=recv2,
            device_id=in_line(z), device_id_type=MESH,
        )

    def done_copy(s):
        return pltpu.make_async_remote_copy(
            src_ref=done.at[mine], dst_ref=done.at[mine], send_sem=send3, recv_sem=recv3,
            device_id=in_plane(s), device_id_type=MESH,
        )

    def weight_copy(dr, dc):
        return pltpu.make_async_remote_copy(
            src_ref=w_own, dst_ref=w_all.at[place(-dr, -dc)],
            send_sem=send_w.at[place(dr, dc)], recv_sem=recv_w.at[place(-dr, -dc)],
            device_id=(fr + dr, fc + dc), device_id_type=MESH,
        )

    def landed(ref, slots, sem):
        view = ref.at[pl.ds(0, slots)]
        pltpu.make_async_copy(view, view, sem).wait()

    for j in range(PIECES):
        @pl.when(me != REDUCERS[j])
        def _():
            piece_copy(j).start()

    @pl.when(reduces)
    def _():
        raw[me] = pay[mine]
        s = lax.broadcasted_iota(i32, (PLANE, 1, LANES), 0)
        holder = (plane_row + (s >> 3)) * N_FCOL + plane_col + (s & 7)
        landed(raw, PLANE - 1, recv1)
        values = raw[...]
        for b in range(NBLK):
            part[b : b + 1, :] = jnp.sum(jnp.where(holder == order[b], values, 0.0), axis=0)
        for z in range(DEPTH):
            @pl.when(my_z != z)
            def _():
                line_copy(z).start()

        line[my_z] = part[...]
        landed(line, DEPTH - 1, recv2)
        done[mine] = jnp.sum(line[...], axis=0)
        for s in PEERS:
            @pl.when(me != s)
            def _():
                done_copy(s).start()

        landed(done, PIECES - 1, recv3)

    @pl.when(jnp.logical_not(reduces))
    def _():
        landed(done, PIECES, recv3)

    for load in loads[4:]:
        load.wait()

    def value(v):
        return jnp.concatenate([done[2 * v], done[2 * v + 1]], 0)

    s1, s2, t = value(2).astype(i32), value(3).astype(i32), value(4).astype(i32)
    first, second = s1 * NT + t, s2 * NT + t

    def pick(part, index):
        lane, row = index & 127, index >> 7
        bits = [(row & (1 << b)) != 0 for b in range(6)]
        stack = []
        for n in range(GAIN_ROWS):
            values = jnp.broadcast_to(gain[2 * n + part : 2 * n + part + 1, :], (SUB, LANES))
            found, level = take_lanes(values, lane), 0
            while stack and stack[-1][0] == level:
                found = jnp.where(bits[level], found, stack.pop()[1])
                level += 1
            stack.append((level, found))
        return stack[0][1]

    scale = 0.5 / math.sqrt(K)
    v_r, v_i = value(0), value(1)
    g1r, g1i = pick(0, first), pick(1, first)
    g2r, g2i = pick(0, second), pick(1, second)
    real_gain = g1r * g2r + g1i * g2i
    imag_gain = g1i * g2r - g1r * g2i
    w_own[0] = scale * (v_r * real_gain - v_i * imag_gain)
    w_own[1] = scale * (v_r * imag_gain + v_i * real_gain)
    for dr, dc in AROUND:
        @pl.when(inside(dr, dc))
        def _():
            weight_copy(dr, dc).start()

    def station(ref):
        total = jnp.zeros((SUB, LANES), i32)
        for row in range(4):
            cells = jnp.broadcast_to(ref[row : row + 1, :], (SUB, LANES))
            one = take_lanes(cells, s1 & 127)
            two = take_lanes(cells, s2 & 127)
            total = total + jnp.where((s1 >> 7) == row, one, 0) - jnp.where((s2 >> 7) == row, two, 0)
        return total

    u, v = station(ucell), station(vcell)
    uv_ref[0] = u
    uv_ref[1] = v
    mid_c, mid_s = circle(u * (fr * (2 * R) + R - 1) + v * (2 * (fc * C + C // 2)))

    def turn(place_of, w_r, w_i):
        w_ref[2 * place_of] = w_r * mid_c - w_i * mid_s
        w_ref[2 * place_of + 1] = w_r * mid_s + w_i * mid_c

    turn(4, w_own[0], w_own[1])

    low = lax.broadcasted_iota(i32, (LOW, LANES), 0)
    step = lax.broadcasted_iota(i32, (SUB, LANES), 0) + 1

    for n, cells in enumerate((uv_ref[0], uv_ref[1])):
        for i in range(1, LOW // SUB):
            spin[n, i - 1, 0], spin[n, i - 1, 1] = circle(cells * (2 * SUB * i))

    def fan(n, g, c, s):
        cos, sin = [c], [s]
        for i in range(LOW // SUB - 1):
            bc, bs = spin[n, i, 0, pl.ds(g, 1), :], spin[n, i, 1, pl.ds(g, 1), :]
            cos.append(c * bc - s * bs)
            sin.append(s * bc + c * bs)
        return jnp.concatenate(cos, 0), jnp.concatenate(sin, 0)

    def row_tables(g):
        u = uv_ref[0, pl.ds(g, 1), :]
        v = uv_ref[1, pl.ds(g, 1), :]
        lc, ls = fan(0, g, *circle(u * (2 * step - 1 + HALF)))
        hc, hs = circle(u * (2 * LOW * step))
        turn_u[0] = hc
        turn_u[1] = hs

        def put(block, c, s):
            at = slice((block + 8) * LOW, (block + 9) * LOW)
            rows_c[g, at, :] = c.astype(bf16)
            rows_s[g, at, :] = s.astype(bf16)
            if block >= 6:
                rim_wave[0, g, (block - 6) * LOW : (block - 5) * LOW, :] = c
                rim_wave[1, g, (block - 6) * LOW : (block - 5) * LOW, :] = s

        put(0, lc, ls)
        for h in range(1, 9):
            bc, bs = turn_u[0, h - 1 : h, :], turn_u[1, h - 1 : h, :]
            cc, ss, cs, sc = lc * bc, ls * bs, lc * bs, ls * bc
            put(-h, cc + ss, sc - cs)
            if h < 8:
                put(h, cc - ss, sc + cs)
        lc, ls = fan(1, g, *circle(v * (2 * step - 2)))
        wave_v[0, g] = lc
        wave_v[1, g] = ls
        hc, hs = circle(v * (2 * LOW * step))
        turn_v[0, g] = hc
        turn_v[1, g] = hs

    def prepare(n, carry):
        row_tables(n)
        return carry

    lax.fori_loop(0, GROUPS, prepare, 0)

    lowf = low.astype(f32)

    def turned(g, h, real, imag):
        bc, bs = turn_v[0, g, h - 1 : h, :], turn_v[1, g, h - 1 : h, :]
        rc, ix, rs, ic = real * bc, imag * bs, real * bs, imag * bc
        return {h: (rc - ix, ic + rs), -h: (rc + ix, ic - rs)}

    def weighted(g, f, lc, ls):
        w_r, w_i = w_ref[2 * f, pl.ds(g, 1), :], w_ref[2 * f + 1, pl.ds(g, 1), :]
        return w_r * lc - w_i * ls, w_r * ls + w_i * lc

    def keep(g, spot, block, own, plain):
        at = slice(block * LOW, (block + 1) * LOW)
        if own is not None:
            cols_a[spot, g, at, :] = own[0].astype(bf16)
            cols_b[spot, g, at, :] = own[1].astype(bf16)
        if plain is not None:
            plain_c[spot, g, at, :] = plain[0].astype(bf16)
            plain_s[spot, g, at, :] = plain[1].astype(bf16)

    def columns(g, spot):
        blocks = (INNER, OUTER)[spot]
        lc, ls = wave_v[0, g], wave_v[1, g]
        z_r, z_i = weighted(g, 4, lc, ls)
        plain = {0: (lc, ls)}
        own = {0: (z_r, z_i)}
        for h in sorted({abs(b) for b in blocks} - {0}):
            plain.update(turned(g, h, lc, ls))
            if h < 7:
                own.update(turned(g, h, z_r, z_i))
        for n, b in enumerate(blocks):
            keep(g, spot, n, own[b] if -7 < b < 6 else None, plain[b])

    def inner(g, carry):
        columns(g, 0)
        return carry

    lax.fori_loop(0, GROUPS, inner, 0)

    def whole(ref, at=None):
        return jnp.concatenate([ref[g] if at is None else ref[at, g] for g in range(GROUPS)], 1)

    def times(rows, cols):
        return lax.dot_general(rows, cols, (((1,), (1,)), ((), ())), preferred_element_type=f32)

    flip = SUB - 1 - lax.broadcasted_iota(i32, (SUB, LANES), 0)

    d = lax.broadcasted_iota(i32, (M, 1), 0).astype(f32)
    t_own = (2 * M - 0.5 - d) * (1 / (2 * M))
    t_next = (d + 0.5) * (1 / (2 * M))
    def edges(g, side):
        for half in range(M // LOW):
            at_half = slice(half * LOW, (half + 1) * LOW)
            c, s = rim_wave[0, g, at_half, :], rim_wave[1, g, at_half, :]
            for f, sign, at in ((side, -1.0, half * LOW), (6 + side, 1.0, M + half * LOW)):
                w_r, w_i = w_ref[2 * f, pl.ds(g, 1), :], w_ref[2 * f + 1, pl.ds(g, 1), :]
                if sign > 0:
                    real, imag = w_r * c - w_i * s, w_r * s + w_i * c
                else:
                    real, imag = w_r * c + w_i * s, w_i * c - w_r * s
                edge_r[g, at : at + LOW, :] = real.astype(bf16)
                edge_i[g, at : at + LOW, :] = imag.astype(bf16)

    def lay(even, odd):
        down = even - odd
        up = even + odd
        rim[0] = up[EDGE:]
        rim[1] = down[EDGE:]
        centre[HALF : R - M, :] = down[:EDGE]
        for i in range(EDGE // SUB):
            for k in range(WIDE // LANES):
                at = slice(k * LANES, (k + 1) * LANES)
                tile = jnp.take_along_axis(up[i * SUB : (i + 1) * SUB, at], flip, axis=0, mode="promise_in_bounds")
                centre[HALF - (i + 1) * SUB : HALF - i * SUB, at] = tile

    lay(times(whole(rows_c), whole(cols_a, 0)), times(whole(rows_s), whole(cols_b, 0)))
    for g in range(GROUPS):
        columns(g, 1)

    def come(dr, dc):
        @pl.when(inside(dr, dc))
        def _():
            slot_of = w_all.at[place(dr, dc)]
            pltpu.make_async_copy(slot_of, slot_of, recv_w.at[place(dr, dc)]).wait()

    for dr, dc in NEAR:
        come(dr, dc)
    for dr, dc in NEAR:
        turn(place(dr, dc), w_all[place(dr, dc), 0], w_all[place(dr, dc), 1])
    for g in range(GROUPS):
        edges(g, 1)
    strip = times(whole(edge_r), whole(plain_c, 0)) - times(whole(edge_i), whole(plain_s, 0))
    top = rim[0] * t_own + strip[:M] * t_next
    centre[R - M :, :] = rim[1] * t_own + strip[M:] * t_next
    for i in range(M // SUB):
        for k in range(WIDE // LANES):
            at = slice(k * LANES, (k + 1) * LANES)
            tile = jnp.take_along_axis(top[i * SUB : (i + 1) * SUB, at], flip, axis=0, mode="promise_in_bounds")
            centre[M - (i + 1) * SUB : M - i * SUB, at] = tile

    @pl.when(reduces)
    def _():
        landed(pay, PIECES - 1, send1)
        landed(line, DEPTH - 1, send2)
        landed(sent, PLANE - 1, send3)

    @pl.when(jnp.logical_not(reduces))
    def _():
        landed(pay, PIECES, send1)

    for dr, dc in AROUND:
        @pl.when(inside(dr, dc))
        def _():
            weight_copy(dr, dc).wait_send()

    for dr, dc in FAR:
        come(dr, dc)
    for dr, dc in FAR:
        turn(place(dr, dc), w_all[place(dr, dc), 0], w_all[place(dr, dc), 1])


def image_kernel(
    w_ref, wave_v, turn_v, rim_wave, rows_c, rows_s, cols_a, cols_b, plain_c, plain_s, centre, mid_r, mid_i, out_hbm,
    edge_a, edge_b, edge_r, edge_i, image, out_sem,
):
    f32, i32, bf16 = jnp.float32, jnp.int32, jnp.bfloat16

    def store(n, source, rows, cols):
        copy = pltpu.make_async_copy(source, out_hbm.at[pl.ds(*rows), pl.ds(*cols)], out_sem.at[n])
        copy.start()
        return copy

    stores = [store(0, centre, (0, R), (LANES, WIDE))]
    low = lax.broadcasted_iota(i32, (LOW, LANES), 0)
    lowf = low.astype(f32)

    def turned(g, h, real, imag):
        bc, bs = turn_v[0, g, h - 1 : h, :], turn_v[1, g, h - 1 : h, :]
        rc, ix, rs, ic = real * bc, imag * bs, real * bs, imag * bc
        return {h: (rc - ix, ic + rs), -h: (rc + ix, ic - rs)}

    def weighted(g, f, lc, ls):
        w_r, w_i = w_ref[2 * f, pl.ds(g, 1), :], w_ref[2 * f + 1, pl.ds(g, 1), :]
        return w_r * lc - w_i * ls, w_r * ls + w_i * lc

    def keep(g, block, own):
        at = slice(block * LOW, (block + 1) * LOW)
        edge_a[g, at, :] = own[0].astype(bf16)
        edge_b[g, at, :] = own[1].astype(bf16)

    def shared(g):
        lc, ls = wave_v[0, g], wave_v[1, g]
        z_r, z_i = weighted(g, 4, lc, ls)
        for f, side in ((3, (-8, -7)), (5, (6, 7))):
            s_r, s_i = weighted(g, f, lc, ls)
            d_r, d_i = z_r - s_r, z_i - s_i
            for b in side:
                start = (b + 8) * LOW
                if b < 0:
                    taper = (lowf + (start + M + 0.5)) * (1 / (2 * M))
                else:
                    taper = (C + M - 0.5 - start - lowf) * (1 / (2 * M))
                keep(g, MARGIN.index(b), turned(g, abs(b), s_r + taper * d_r, s_i + taper * d_i)[b])

    def edges(g, side):
        for half in range(M // LOW):
            at_half = slice(half * LOW, (half + 1) * LOW)
            c, s = rim_wave[0, g, at_half, :], rim_wave[1, g, at_half, :]
            for f, sign, at in ((side, -1.0, half * LOW), (6 + side, 1.0, M + half * LOW)):
                w_r, w_i = w_ref[2 * f, pl.ds(g, 1), :], w_ref[2 * f + 1, pl.ds(g, 1), :]
                if sign > 0:
                    real, imag = w_r * c - w_i * s, w_r * s + w_i * c
                else:
                    real, imag = w_r * c + w_i * s, w_i * c - w_r * s
                edge_r[side // 2, g, at : at + LOW, :] = real.astype(bf16)
                edge_i[side // 2, g, at : at + LOW, :] = imag.astype(bf16)

    def whole(ref, at=None):
        return jnp.concatenate([ref[g] if at is None else ref[at, g] for g in range(GROUPS)], 1)

    def times(rows, cols):
        return lax.dot_general(rows, cols, (((1,), (1,)), ((), ())), preferred_element_type=f32)

    d = lax.broadcasted_iota(i32, (M, 1), 0).astype(f32)
    t_own = (2 * M - 0.5 - d) * (1 / (2 * M))
    t_next = (d + 0.5) * (1 / (2 * M))
    flip = SUB - 1 - lax.broadcasted_iota(i32, (SUB, LANES), 0)

    def lay(down, up, start):
        to = slice(start, start + LANES)
        image[HALF : R - M, to] = down[:EDGE]
        for i in range(EDGE // SUB):
            tile = jnp.take_along_axis(up[i * SUB : (i + 1) * SUB], flip, axis=0, mode="promise_in_bounds")
            image[HALF - (i + 1) * SUB : HALF - i * SUB, to] = tile

    def seam(up, down, strip, start):
        to = slice(start, start + LANES)
        top = up * t_own + strip[:M] * t_next
        image[R - M :, to] = down * t_own + strip[M:] * t_next
        for i in range(M // SUB):
            tile = jnp.take_along_axis(top[i * SUB : (i + 1) * SUB], flip, axis=0, mode="promise_in_bounds")
            image[M - (i + 1) * SUB : M - i * SUB, to] = tile

    for g in range(GROUPS):
        shared(g)
        for side in (0, 2):
            edges(g, side)

    column = lax.broadcasted_iota(i32, (1, WIDE), 1)
    column = jnp.where(column < LANES, column, column + C - WIDE).astype(f32)
    t_mid = jnp.minimum(jnp.minimum((column + (M + 0.5)) * (1 / (2 * M)), (C + M - 0.5 - column) * (1 / (2 * M))), 1.0)
    t_left = jnp.maximum(M - 0.5 - column, 0.0) * (1 / (2 * M))
    t_right = jnp.maximum(column - (C - M - 0.5), 0.0) * (1 / (2 * M))

    def strips():
        real = jnp.concatenate([whole(edge_r, 0), whole(mid_r), whole(edge_r, 1)], 0)
        imag = jnp.concatenate([whole(edge_i, 0), whole(mid_i), whole(edge_i, 1)], 0)
        return times(real, whole(plain_c, 1)) - times(imag, whole(plain_s, 1))

    def outer_cols(inner_ref, edge_ref):
        parts = []
        for g in range(GROUPS):
            own = inner_ref[1, g]
            parts.append(jnp.concatenate([edge_ref[g, : 2 * LOW], own[2 * LOW : 6 * LOW], edge_ref[g, 2 * LOW :]], 0))
        return jnp.concatenate(parts, 1)

    even = times(whole(rows_c), outer_cols(cols_a, edge_a))
    odd = times(whole(rows_s), outer_cols(cols_b, edge_b))
    down, up = even - odd, even + odd
    for k, start in ((0, 0), (1, C - LANES)):
        at = slice(k * LANES, (k + 1) * LANES)
        lay(down[:EDGE, at], up[:EDGE, at], start)
        stores.append(store(1 + k, image.at[pl.ds(M, 2 * EDGE), pl.ds(start, LANES)], (M, 2 * EDGE), (start, LANES)))
    strip = strips()
    strip = strip[: 2 * M] * t_left + strip[2 * M : 4 * M] * t_mid + strip[4 * M :] * t_right
    for k, start in ((0, 0), (1, C - LANES)):
        at = slice(k * LANES, (k + 1) * LANES)
        seam(up[EDGE:, at], down[EDGE:, at], strip[:, at], start)
    for n, row in ((3, 0), (5, R - M)):
        for k, start in ((0, 0), (1, C - LANES)):
            stores.append(store(n + k, image.at[pl.ds(row, M), pl.ds(start, LANES)], (row, M), (start, LANES)))
    for copy in stores:
        copy.wait()


def tile_of(order, vis, pairs, slot, ucell, vcell, gain):
    dma, vmem = pltpu.SemaphoreType.DMA, pltpu.VMEM
    f32, i32, bf16 = jnp.float32, jnp.int32, jnp.bfloat16
    inside = pl.BlockSpec(memory_space=pltpu.VMEM)
    kept = (
        vmem((18, SUB, LANES), f32),
        vmem((2, GROUPS, LOW, LANES), f32),
        vmem((2, GROUPS, SUB, LANES), f32),
        vmem((2, GROUPS, M, LANES), f32),
        vmem((GROUPS, HALF, LANES), bf16),
        vmem((GROUPS, HALF, LANES), bf16),
        vmem((2, GROUPS, WIDE, LANES), bf16),
        vmem((2, GROUPS, WIDE, LANES), bf16),
        vmem((2, GROUPS, WIDE, LANES), bf16),
        vmem((2, GROUPS, WIDE, LANES), bf16),
        vmem((R, WIDE), f32),
        vmem((GROUPS, 2 * M, LANES), bf16),
        vmem((GROUPS, 2 * M, LANES), bf16),
    )
    tables = pl.pallas_call(
        exchange_kernel,
        out_shape=kept,
        in_specs=[pl.BlockSpec(memory_space=pltpu.HBM)] * 7,
        out_specs=(inside,) * len(kept),
        scratch_shapes=[
            pltpu.SMEM((N_FROW * N_FCOL,), i32),
            vmem((2, BLOCK), f32),
            vmem((2, BLOCK), i32),
            vmem((1, BLOCK), i32),
            vmem((4, LANES), i32),
            vmem((4, LANES), i32),
            vmem((2 * GAIN_ROWS, LANES), f32),
            vmem((PIECES, 1, LANES), f32),
            vmem((PLANE, 1, LANES), f32),
            vmem((NBLK, LANES), f32),
            vmem((DEPTH, NBLK, LANES), f32),
            vmem((PIECES, NBLK, LANES), f32),
            vmem((2, SUB, LANES), f32),
            vmem((9, 2, SUB, LANES), f32),
            vmem((2, SUB, LANES), i32),
            vmem((2, SUB, LANES), f32),
            vmem((2, LOW // SUB - 1, 2, SUB, LANES), f32),
            vmem((2, M, WIDE), f32),
            vmem((PLANE - 1, NBLK, LANES), f32),
            dma((7,)), dma, dma, dma, dma, dma, dma, dma((9,)), dma((9,)),
        ],
        compiler_params=pltpu.CompilerParams(collective_id=0, has_side_effects=True, vmem_limit_bytes=24 * 1024 * 1024),
        name="exchange",
    )(*[pltpu.with_memory_space_constraint(x, pltpu.HBM) for x in (order, vis, pairs, slot, ucell, vcell, gain)])
    return pl.pallas_call(
        image_kernel,
        out_shape=jax.ShapeDtypeStruct((R, C), f32),
        in_specs=[inside] * len(kept),
        out_specs=pl.BlockSpec(memory_space=pl.ANY),
        scratch_shapes=[
            vmem((GROUPS, 2 * M, LANES), bf16),
            vmem((GROUPS, 2 * M, LANES), bf16),
            vmem((2, GROUPS, 2 * M, LANES), bf16),
            vmem((2, GROUPS, 2 * M, LANES), bf16),
            vmem((R, C), f32),
            dma((7,)),
        ],
        compiler_params=pltpu.CompilerParams(vmem_limit_bytes=24 * 1024 * 1024),
        name="image",
    )(*tables)


def shards(vis, station_pairs, visibility_time_slot, station_u_cells, station_v_cells, facet_station_gains, holder_device_order):
    gains = facet_station_gains.reshape(2, GAIN_ROWS, LANES).transpose(1, 0, 2).reshape(2 * GAIN_ROWS, LANES)
    return tile_of(
        holder_device_order, vis, station_pairs, visibility_time_slot.reshape(1, BLOCK),
        station_u_cells.reshape(4, LANES), station_v_cells.reshape(4, LANES), gains,
    )


def solution(mesh):
    return jax.shard_map(
        shards,
        mesh=mesh,
        in_specs=(
            P(None, ("frow", "fcol")),
            P(None, ("frow", "fcol")),
            P(("frow", "fcol")),
            P(),
            P(),
            P("frow", "fcol", None, None),
            P(),
        ),
        out_specs=P("frow", "fcol"),
        check_vma=False,
    )
```
